32 devices in a mesh: dp: 4 (over z), shard: 8 (over y, x, core).
Axes of the slice: x: 2, y: 2, z: 4, core: 2. Of those that a mesh axis runs over, the one named last changes fastest.
Arguments:
- hidden: bfloat16 [192, 256, 1024], P(('dp', 'shard')), may hold values from -40 to 40, as said below
- lengths: int32 [192], replicated, may hold values from 16 to 256
- dealing: int32 [192], replicated, may hold values from 0 to 191, each once
- candidates: int32 [192, 64], P(('dp', 'shard')), may hold values from 0 to 131071
- index_rows: bfloat16 [131072, 1024], P(('dp', 'shard')), may hold values from -6 to 6
- qkv_weight: bfloat16 [1024, 3072], replicated, may hold values from -0.1875 to 0.1875
- qkv_bias: float32 [3072], replicated, may hold values from -3 to 3
- out_weight: bfloat16 [1024, 1024], replicated, may hold values from -0.1875 to 0.1875
- out_bias: float32 [1024], replicated, may hold values from -3 to 3
- norm_gain: float32 [1024], replicated, may hold values from 0.25 to 1.75
- norm_shift: float32 [1024], replicated, may hold values from -3 to 3
Outputs:
- scores: float32 [192, 64], P(('dp', 'shard'))
The draws below stay inside these ranges and needn't reach their ends.
Inputs may be any that keep to these rules, and one draw needn't show every extreme that they name: dealing names every text once. `hidden`: token states of order one, some much larger.
All inputs are finite; a program needn't handle non-finite values.
Results may differ from the reference program's by a relative error of at most 0.0044.
Values may be sent and summed in bfloat16 or wider, within the bound.
A program may use at most 128 MiB of HBM per device.

```python
import jax
import jax.numpy as jnp
from jax import lax

D = 1024
HEADS = 16
HEAD = 64
LMAX = 256
K = 64
TEXTS = 192
ROWS = 131072


def draw_hidden(key, part):
    shape = (TEXTS, LMAX, D)
    values = jnp.clip(jax.random.normal(key, shape, jnp.float32), -6.0, 6.0)
    return values.astype(jnp.bfloat16)


def with_ends(array, stream_key, smallest, top_value):
    place = [jax.random.randint(jax.random.fold_in(stream_key, axis), (), 0, length) for axis, length in enumerate(array.shape)]
    widest = array.shape.index(max(array.shape))
    next_to = place[:widest] + [(place[widest] + 1) % array.shape[widest]] + place[widest + 1:]
    return array.at[tuple(place)].set(smallest).at[tuple(next_to)].set(top_value)


def level_of(key, dims, cuts, low, top_value):
    loudness = 1.0
    for dim, blocks in cuts:
        heights = jax.random.uniform(jax.random.fold_in(jax.random.fold_in(key, 6), dim), (blocks,), jnp.float32, low / len(cuts), top_value / len(cuts))
        loudness = loudness * jnp.repeat(jnp.exp(heights), dims[dim] // blocks).reshape((-1,) + (1,) * (len(dims) - 1 - dim))
    return loudness


def bell_draw(stream_key, dims, width, most, shards=(), kind=jnp.bfloat16):
    entries = width * jax.random.normal(stream_key, dims, jnp.float32)
    if shards:
        entries = entries * level_of(stream_key, dims, shards, -0.22, 0.18)
    return jnp.clip(entries, -most, most).astype(kind)


def setup_inputs(seed: int = 0) -> dict:
    seeds = jax.random.split(jax.random.key(seed), 12)
    return {
        "hidden": draw_hidden(jax.random.fold_in(seeds[11], 71), 0),
        "lengths": with_ends(jax.random.randint(seeds[1], (TEXTS,), LMAX // 16, LMAX + 1), jax.random.fold_in(seeds[1], 1), LMAX // 16, LMAX).astype(jnp.int32),
        "dealing": jax.random.permutation(seeds[2], TEXTS).astype(jnp.int32),
        "candidates": with_ends(jax.random.randint(seeds[3], (TEXTS, K), 0, ROWS), jax.random.fold_in(seeds[3], 1), 0, ROWS - 1).astype(jnp.int32),
        "index_rows": bell_draw(seeds[4], (ROWS, D), 1.0, 6.0, ((0, 32),)),
        "qkv_weight": bell_draw(seeds[5], (D, 3 * D), D ** -0.5, 0.1875),
        "qkv_bias": bell_draw(seeds[6], (3 * D,), 0.5, 3.0, (), jnp.float32),
        "out_weight": bell_draw(seeds[7], (D, D), D ** -0.5, 0.1875),
        "out_bias": bell_draw(seeds[8], (D,), 0.5, 3.0, (), jnp.float32),
        "norm_gain": jnp.clip(1.0 + 0.15 * jax.random.normal(seeds[9], (D,), jnp.float32), 0.25, 1.75),
        "norm_shift": bell_draw(seeds[10], (D,), 0.5, 3.0, (), jnp.float32),
    }


def encode_text(states, text_len, qkv_weight, qkv_bias, out_weight, out_bias, norm_gain, norm_shift):
    model_width = states.shape[1]
    seq_len = states.shape[0]
    qkv = (jnp.dot(states, qkv_weight, preferred_element_type=jnp.float32) + qkv_bias).astype(jnp.bfloat16)
    q_part = qkv[:, :model_width].reshape(seq_len, HEADS, HEAD).astype(jnp.float32)
    k_part = qkv[:, model_width:2 * model_width].reshape(seq_len, HEADS, HEAD).astype(jnp.float32)
    v_part = qkv[:, 2 * model_width:].reshape(seq_len, HEADS, HEAD).astype(jnp.float32)
    logits = jnp.einsum('qhd,khd->hqk', q_part, k_part) * (1.0 / HEAD ** 0.5)
    positions = jnp.arange(seq_len, dtype=jnp.int32)
    key_valid = positions < text_len
    logits = jnp.where(key_valid[None, None, :], logits, -1e+30)
    peak = lax.optimization_barrier(jnp.max(logits, axis=-1, keepdims=True))
    weights = jnp.exp(logits - peak)
    probs = (weights / lax.optimization_barrier(jnp.sum(weights, axis=-1, keepdims=True))).astype(jnp.bfloat16)
    context = jnp.einsum('hqk,khd->qhd', probs.astype(jnp.float32), v_part)
    context = context.reshape(seq_len, model_width).astype(jnp.bfloat16)
    resid = states.astype(jnp.float32) + jnp.dot(context, out_weight, preferred_element_type=jnp.float32) + out_bias
    centre = lax.optimization_barrier(jnp.mean(resid, axis=-1, keepdims=True))
    spread = lax.optimization_barrier(jnp.mean((resid - centre) ** 2, axis=-1, keepdims=True))
    normed = (resid - centre) * lax.rsqrt(spread + 1e-05) * norm_gain + norm_shift
    pooled = lax.optimization_barrier(jnp.sum(jnp.where(key_valid[:, None], normed, 0.0), axis=0)) / text_len.astype(jnp.float32)
    queries = pooled * lax.rsqrt(jnp.sum(pooled * pooled) + 1e-06)
    return queries.astype(jnp.bfloat16)

def reference(hidden, lengths, dealing, candidates, index_rows, qkv_weight, qkv_bias, out_weight, out_bias, norm_gain, norm_shift):
    slot_lens = lengths[dealing]

    def one_slot(pair):
        return encode_text(pair[0], pair[1], qkv_weight, qkv_bias, out_weight, out_bias, norm_gain, norm_shift)
    slot_queries = lax.map(one_slot, (hidden, slot_lens))
    text_queries = jnp.zeros_like(slot_queries).at[dealing].set(slot_queries)

    def one_text(pair):
        fetched = index_rows[pair[1]]
        return jnp.dot(fetched, pair[0], preferred_element_type=jnp.float32)
    return lax.map(one_text, (text_queries, candidates))
```

```python
import functools

import jax
import jax.numpy as jnp
from jax import lax
from jax.experimental import pallas as pl
from jax.experimental.pallas import tpu as pltpu
from jax.sharding import PartitionSpec as P

HEADS = 16
HEAD = 64
LANES = 128
SLOTS = 8
GRAIN = 16
UNIT = 128
PACK = 4
ID_ROW = 6
LEN_ROW = 7


def attend(qkv_ref, context_ref, start, rows, keys_count, text_len):
    width = context_ref.shape[1]
    queries, keys = pl.ds(start, rows), pl.ds(start, keys_count)
    lane = lax.broadcasted_iota(jnp.int32, (keys_count, LANES), 1)
    place = lax.broadcasted_iota(jnp.int32, (keys_count, LANES), 0)
    first = lane < HEAD
    valid = place < text_len
    key_valid = lax.broadcasted_iota(jnp.int32, (1, keys_count), 1) < text_len
    zero = jnp.zeros((keys_count, LANES), jnp.bfloat16)
    ones = jnp.ones((keys_count, LANES), jnp.bfloat16)
    ones_a, ones_b = jnp.where(first, ones, zero), jnp.where(first, zero, ones)
    first_valid, second_valid = first & valid, jnp.logical_not(first) & valid
    logits = []
    for base in range(0, width, LANES):
        q2 = qkv_ref[queries, base : base + LANES]
        k2 = qkv_ref[keys, width + base : width + base + LANES]
        for part in (jnp.where(first, k2, zero), jnp.where(first, zero, k2)):
            logits.append(
                lax.dot_general(
                    q2, part, (((1,), (1,)), ((), ())), preferred_element_type=jnp.float32
                )
            )
    probs = []
    for part in logits:
        part = jnp.where(key_valid, part, -1e30)
        peak = jnp.max(part, axis=-1, keepdims=True)
        probs.append(jnp.exp(part - peak).astype(jnp.bfloat16))
    for pair, base in enumerate(range(0, width, LANES)):
        v2 = qkv_ref[keys, 2 * width + base : 2 * width + base + LANES]
        both = jnp.concatenate(probs[2 * pair : 2 * pair + 2], axis=1)
        values = jnp.concatenate(
            [
                jnp.concatenate([jnp.where(first_valid, v2, zero), ones_a], axis=1),
                jnp.concatenate([jnp.where(second_valid, v2, zero), ones_b], axis=1),
            ],
            axis=0,
        )
        mixed = jnp.dot(both, values, preferred_element_type=jnp.float32)
        context_ref[queries, base : base + LANES] = (mixed[:, :LANES] / mixed[:, LANES:]).astype(
            jnp.bfloat16
        )


def project(states, qkv_weight, bias_ref, qkv_ref, rows, part):
    width = states.shape[1]
    chunk = 512
    for start in range(part * width, (part + 1) * width, chunk):
        cols = slice(start, start + chunk)
        out = (
            jnp.dot(states, qkv_weight[:, cols], preferred_element_type=jnp.float32)
            + bias_ref[:, cols]
        )
        if part == 0:
            out = out * (1.0 / HEAD**0.5)
        qkv_ref[rows, cols] = out.astype(jnp.bfloat16)


def normalise(states, context, out_weight, out_bias_ref):
    resid = (
        states.astype(jnp.float32)
        + jnp.dot(context, out_weight[...], preferred_element_type=jnp.float32)
        + out_bias_ref[...]
    )
    centre = jnp.mean(resid, axis=-1, keepdims=True)
    resid = resid - centre
    spread = jnp.mean(resid * resid, axis=-1, keepdims=True)
    return resid * lax.rsqrt(spread + 1e-05)


def embed(total, count, gain_ref, shift_ref):
    pooled = total / count * gain_ref[...] + shift_ref[...]
    return pooled * lax.rsqrt(jnp.sum(pooled * pooled, axis=-1, keepdims=True) + 1e-06)


def encode_kernel(
    shard_count,
    lengths_ref,
    dealing_ref,
    cand_ref,
    qkv_bias_ref,
    out_bias_ref,
    gain_ref,
    shift_ref,
    hidden_hbm,
    qkv_weight_hbm,
    out_weight_hbm,
    index_hbm,
    queries_ref,
    meta_ref,
    long_states,
    qkv_weight,
    out_weight,
    index_rows,
    states_ref,
    qkv_ref,
    context_ref,
    fold_ref,
    load_sems,
    state_sems,
):
    text_dev, seq_len, width = hidden_hbm.shape
    me = lax.axis_index("dp") * shard_count + lax.axis_index("shard")
    texts = [dealing_ref[me * text_dev + slot] for slot in range(text_dev)]
    counts = [lengths_ref[text] for text in texts]
    longest, long_count, long_text = jnp.int32(0), counts[0], texts[0]
    for slot in range(1, text_dev):
        more = counts[slot] > long_count
        longest = jnp.where(more, slot, longest)
        long_count = jnp.where(more, counts[slot], long_count)
        long_text = jnp.where(more, texts[slot], long_text)
    starts, sizes = [], []
    total_rows = jnp.int32(0)
    for slot in range(text_dev):
        size = jnp.where(longest == slot, 0, (counts[slot] + GRAIN - 1) // GRAIN * GRAIN)
        starts.append(total_rows)
        sizes.append(size)
        total_rows = total_rows + size

    def state_copy(slot):
        size = pl.multiple_of(sizes[slot], GRAIN)
        return pltpu.make_async_copy(
            hidden_hbm.at[slot, pl.ds(0, size)],
            states_ref.at[pl.ds(pl.multiple_of(starts[slot], GRAIN), size)],
            state_sems.at[slot],
        )

    loads = [
        pltpu.make_async_copy(
            qkv_weight_hbm.at[:, pl.ds(part * width, width)],
            qkv_weight.at[:, pl.ds(part * width, width)],
            load_sems.at[part],
        )
        for part in range(3)
    ]
    loads.append(pltpu.make_async_copy(out_weight_hbm, out_weight, load_sems.at[3]))
    loads.append(pltpu.make_async_copy(hidden_hbm.at[longest], long_states, load_sems.at[4]))
    loads.append(pltpu.make_async_copy(index_hbm, index_rows, load_sems.at[5]))

    for slot in range(text_dev):
        pl.when(longest != slot)(lambda slot=slot: state_copy(slot).start())
    for load in loads[:3]:
        load.start()
    meta_ref[...] = jnp.zeros_like(meta_ref)
    meta_ref[:text_dev, : cand_ref.shape[1]] = cand_ref[...]
    meta_ref[ID_ROW : ID_ROW + 1, :] = jnp.full((1, LANES), long_text, jnp.int32)
    meta_ref[LEN_ROW : LEN_ROW + 1, :] = jnp.full((1, LANES), long_count, jnp.int32)
    for slot in range(text_dev):
        pl.when(longest != slot)(lambda slot=slot: state_copy(slot).wait())

    units = (total_rows + UNIT - 1) // UNIT
    full, rest = units // PACK, lax.rem(units, PACK)

    def over_rows(body):
        def step(i, carry):
            body(pl.multiple_of(i * (PACK * UNIT), PACK * UNIT), PACK * UNIT)
            return carry

        lax.fori_loop(0, full, step, 0)
        for size in range(1, PACK):
            pl.when(rest == size)(
                lambda size=size: body(
                    pl.multiple_of(full * (PACK * UNIT), PACK * UNIT), size * UNIT
                )
            )

    for part in range(3):
        loads[part].wait()
        if part == 0:
            for load in loads[3:]:
                load.start()

        def qkv_block(base, size):
            rows = pl.ds(base, size)
            project(states_ref[rows, :], qkv_weight, qkv_bias_ref, qkv_ref, rows, part)

        over_rows(qkv_block)

    def text_step(slot, carry):
        count, start = counts[0], starts[0]
        for other in range(1, text_dev):
            count = jnp.where(slot == other, counts[other], count)
            start = jnp.where(slot == other, starts[other], start)
        start = pl.multiple_of(start, GRAIN)
        small = count <= 128
        large = count > 192
        mine = slot != longest

        @pl.when(mine & small)
        def _():
            attend(qkv_ref, context_ref, start, 128, 128, count)

        @pl.when(mine & jnp.logical_not(small | large))
        def _():
            attend(qkv_ref, context_ref, start, 192, 256, count)

        @pl.when(mine & large)
        def _():
            attend(qkv_ref, context_ref, start, 256, 256, count)

        return carry

    lax.fori_loop(0, text_dev, text_step, 0)

    loads[3].wait()
    slot_id = lax.broadcasted_iota(jnp.int32, (SLOTS, 1), 0)
    start_col = jnp.zeros((SLOTS, 1), jnp.int32)
    count_col = jnp.zeros((SLOTS, 1), jnp.int32)
    for slot in range(text_dev):
        here = slot_id == slot
        start_col = jnp.where(here, starts[slot], start_col)
        count_col = jnp.where(here, jnp.where(longest == slot, 0, counts[slot]), count_col)
    fold_ref[...] = jnp.zeros_like(fold_ref)

    def out_block(base, size):
        rows = pl.ds(base, size)
        normed = normalise(states_ref[rows, :], context_ref[rows, :], out_weight, out_bias_ref)
        row = lax.broadcasted_iota(jnp.int32, (size, 1), 0) + base
        normed = jnp.where(row < total_rows, normed, 0.0).astype(jnp.bfloat16)
        place = lax.broadcasted_iota(jnp.int32, (SLOTS, size), 1) + base - start_col
        member = (place >= 0) & (place < count_col)
        fold_ref[...] += jnp.dot(
            jnp.where(member, 1.0, 0.0).astype(jnp.bfloat16),
            normed,
            preferred_element_type=jnp.float32,
        )

    over_rows(out_block)
    query = embed(
        fold_ref[...], jnp.maximum(count_col, 1).astype(jnp.float32), gain_ref, shift_ref
    )
    query = jnp.where(count_col > 0, query, 0.0)
    pieces = width // LANES
    for slot in range(text_dev):
        for piece in range(pieces):
            queries_ref[slot, piece : piece + 1, :] = query[
                slot : slot + 1, piece * LANES : (piece + 1) * LANES
            ]
    loads[4].wait()
    loads[5].wait()


def finish_kernel(
    dp_count,
    shard_count,
    text_dev,
    dealt_ref,
    qkv_bias_ref,
    out_bias_ref,
    gain_ref,
    shift_ref,
    first_queries,
    meta_ref,
    long_states,
    qkv_weight,
    out_weight,
    index_rows,
    out_ref,
    qkv_ref,
    context_ref,
    fold_ref,
    queries,
    last_queries,
    cands,
    wide_queries,
    slot_queries,
    wide_last,
    last_wide_queries,
    text_queries,
    pick_ref,
    pick_last_ref,
    terms,
    arrived,
    dp_send,
    dp_recv,
    shard_send,
    shard_recv,
    all_send,
    all_recv,
    out_send,
    out_recv,
):
    my_dp, my_shard = lax.axis_index("dp"), lax.axis_index("shard")
    me = my_dp * shard_count + my_shard
    seq_len, width = long_states.shape
    pieces = width // LANES
    devices = dp_count * shard_count
    compact = devices * text_dev

    def dp_peer(off):
        return lax.rem(my_dp + off, dp_count)

    def shard_peer(off):
        return lax.rem(my_shard + off, shard_count)

    def remote(block, send, recv, which, off, device):
        return pltpu.make_async_remote_copy(
            src_ref=block,
            dst_ref=block,
            send_sem=send.at[which, off],
            recv_sem=recv.at[which, off],
            device_id=device,
            device_id_type=pl.DeviceIdType.MESH,
        )

    held = [queries, cands]

    def to_dp(which, off, dp):
        block = held[which].at[my_shard, dp]
        return remote(block, dp_send, dp_recv, which, off, (dp_peer(off), my_shard))

    def to_shard(which, off, shard):
        block = held[which].at[shard]
        return remote(block, shard_send, shard_recv, which, off, (my_dp, shard_peer(off)))

    def dp_start(which):
        for off in range(1, dp_count):
            to_dp(which, off, my_dp).start()

    def dp_finish(which):
        for off in range(1, dp_count):
            to_dp(which, off, lax.rem(my_dp + dp_count - off, dp_count)).wait_recv()

    def shard_start(which):
        for off in range(1, shard_count):
            to_shard(which, off, my_shard).start()

    def shard_finish(which):
        for off in range(1, shard_count):
            to_shard(which, off, lax.rem(my_shard + shard_count - off, shard_count)).wait_recv()

    def sent(which):
        for off in range(1, dp_count):
            to_dp(which, off, my_dp).wait_send()
        for off in range(1, shard_count):
            to_shard(which, off, my_shard).wait_send()

    everyone = [
        (far, off)
        for far in range(dp_count)
        for off in range(shard_count)
        if (far, off) != (0, 0)
    ][::-1]

    def to_all(far, off, dp, shard):
        block = last_queries.at[shard, dp]
        return remote(
            block, all_send, all_recv, far, off, (dp_peer(far), shard_peer(off))
        )

    barrier = pltpu.get_barrier_semaphore()
    for far, off in everyone:
        pl.semaphore_signal(
            barrier,
            inc=1,
            device_id=(dp_peer(far), shard_peer(off)),
            device_id_type=pl.DeviceIdType.MESH,
        )
    queries[my_shard, my_dp] = first_queries[...].astype(jnp.bfloat16)
    cands[my_shard, my_dp] = meta_ref[...]
    text_len = meta_ref[LEN_ROW : LEN_ROW + 1, 0:1]

    states = long_states[...]
    rows = pl.ds(0, seq_len)
    project(states, qkv_weight, qkv_bias_ref, qkv_ref, rows, 0)
    pl.semaphore_wait(barrier, devices - 1)
    dp_start(1)
    dp_start(0)
    project(states, qkv_weight, qkv_bias_ref, qkv_ref, rows, 1)
    project(states, qkv_weight, qkv_bias_ref, qkv_ref, rows, 2)
    dp_finish(1)
    shard_start(1)
    dp_finish(0)
    shard_start(0)

    entry = lax.broadcasted_iota(jnp.int32, (compact, 1), 0)
    block = entry % devices
    texts = ((block % dp_count) * shard_count + block // dp_count) * text_dev + entry // devices
    slot_entry = lax.broadcasted_iota(jnp.int32, (1, compact), 1)
    block = slot_entry // text_dev
    slots = (
        (block % dp_count) * shard_count + block // dp_count
    ) * text_dev + slot_entry % text_dev
    holds = jnp.where(dealt_ref[...] == texts, 1.0, 0.0).astype(jnp.bfloat16)
    natural = lax.broadcasted_iota(jnp.int32, (compact, compact), 0)
    moves = jnp.where(natural == slots, 1.0, 0.0).astype(jnp.bfloat16)
    pick_ref[...] = jnp.dot(holds, moves, preferred_element_type=jnp.float32).astype(jnp.bfloat16)

    attend(qkv_ref, context_ref, 0, seq_len, seq_len, text_len)
    normed = normalise(states, context_ref[...], out_weight, out_bias_ref)
    row = lax.broadcasted_iota(jnp.int32, (seq_len, 1), 0)
    total = jnp.sum(jnp.where(row < text_len, normed, 0.0), axis=0, keepdims=True)
    query = embed(total, text_len.astype(jnp.float32), gain_ref, shift_ref)
    for piece in range(pieces):
        fold_ref[piece : piece + 1, :] = query[:, piece * LANES : (piece + 1) * LANES]
    last_queries[my_shard, my_dp] = fold_ref[...].astype(jnp.bfloat16)
    for far, off in everyone:
        to_all(far, off, my_dp, my_shard).start()

    shard_finish(1)
    shard_finish(0)
    wide_queries[...] = queries[...].astype(jnp.float32).reshape(compact, pieces, LANES)
    for piece in range(pieces):
        slot_queries[:, piece * LANES : (piece + 1) * LANES] = wide_queries[:, piece, :].astype(
            jnp.bfloat16
        )
    ids = cands[...].reshape(devices, SLOTS, LANES)[:, ID_ROW, :]
    diagonal = lax.broadcasted_iota(jnp.int32, (devices, LANES), 0) == lax.broadcasted_iota(
        jnp.int32, (devices, LANES), 1
    )
    ids = jnp.sum(jnp.where(diagonal, ids, 0), axis=0, keepdims=True)[:, :devices]
    pick_last_ref[...] = jnp.where(ids == texts, 1.0, 0.0).astype(jnp.bfloat16)
    first_part = jnp.dot(pick_ref[...], slot_queries[...], preferred_element_type=jnp.float32)

    for far, off in everyone:
        to_all(
            far,
            off,
            lax.rem(my_dp + dp_count - far, dp_count),
            lax.rem(my_shard + shard_count - off, shard_count),
        ).wait_recv()
    wide_last[...] = last_queries[...].astype(jnp.float32).reshape(devices, pieces, LANES)
    for piece in range(pieces):
        last_wide_queries[:, piece * LANES : (piece + 1) * LANES] = wide_last[
            :, piece, :
        ].astype(jnp.bfloat16)
    text_queries[...] = (
        first_part
        + jnp.dot(pick_last_ref[...], last_wide_queries[...], preferred_element_type=jnp.float32)
    ).astype(jnp.bfloat16)

    rows_here = index_rows.shape[0]
    grouped = cands[...].reshape(devices, SLOTS, LANES)
    local = (
        jnp.concatenate([grouped[:, slot, :] for slot in range(text_dev)], axis=0)
        - me * rows_here
    )
    group = local >> 7
    lane = local & (LANES - 1)
    total = jnp.zeros((compact, LANES), jnp.float32)
    rows_step = 1024
    for step in range(rows_here // rows_step):
        scores = lax.dot_general(
            text_queries[...],
            index_rows[step * rows_step : (step + 1) * rows_step, :],
            (((1,), (1,)), ((), ())),
            preferred_element_type=jnp.float32,
        )
        for part in range(rows_step // LANES):
            found = jnp.take_along_axis(
                scores[:, part * LANES : (part + 1) * LANES],
                lane,
                axis=1,
                mode="promise_in_bounds",
            )
            total = jnp.where(group == step * (rows_step // LANES) + part, found, total)

    half = text_dev // 2
    cand_count = LANES // 2
    low = lax.broadcasted_iota(jnp.int32, (half * devices, LANES), 1) < cand_count
    packed = jnp.where(
        low, total[: half * devices], pltpu.roll(total[half * devices :], cand_count, 1)
    )
    for line in range(half):
        terms[:, line, :] = packed[line * devices : (line + 1) * devices]

    def deliver(far, off):
        return pltpu.make_async_remote_copy(
            src_ref=terms.at[shard_peer(off) * dp_count + dp_peer(far)],
            dst_ref=arrived.at[far, off],
            send_sem=out_send.at[far, off],
            recv_sem=out_recv.at[far, off],
            device_id=(dp_peer(far), shard_peer(off)),
            device_id_type=pl.DeviceIdType.MESH,
        )

    for far, off in everyone:
        deliver(far, off).start()
    for which in (0, 1):
        sent(which)
    for far, off in everyone:
        to_all(far, off, my_dp, my_shard).wait_send()
    result = terms[my_shard * dp_count + my_dp]
    for far, off in everyone:
        deliver(far, off).wait_recv()
    for far, off in everyone:
        result = result + arrived[far, off]
    out_ref[:half, :] = result[:half, :cand_count]
    out_ref[half:, :] = result[:half, cand_count:]
    for far, off in everyone:
        deliver(far, off).wait_send()


def shards(
    hidden,
    lengths,
    dealing,
    candidates,
    index_rows,
    qkv_weight,
    qkv_bias,
    out_weight,
    out_bias,
    norm_gain,
    norm_shift,
):
    text_dev, seq_len, width = hidden.shape
    dp_count, shard_count = lax.axis_size("dp"), lax.axis_size("shard")
    devices = dp_count * shard_count
    compact = devices * text_dev
    pieces = width // LANES
    hbm = pl.BlockSpec(memory_space=pl.ANY)
    vmem = pl.BlockSpec(memory_space=pltpu.VMEM)
    smem = pl.BlockSpec(memory_space=pltpu.SMEM)
    small = (qkv_bias[None, :], out_bias[None, :], norm_gain[None, :], norm_shift[None, :])
    room = (text_dev - 1) * seq_len

    first_queries, meta, long_states, qkv_held, out_held, index_held = pl.pallas_call(
        functools.partial(encode_kernel, shard_count),
        in_specs=[smem, smem, *[vmem] * 5, *[hbm] * 4],
        out_specs=[vmem] * 6,
        out_shape=[
            jax.ShapeDtypeStruct((text_dev, pieces, LANES), jnp.float32),
            jax.ShapeDtypeStruct((SLOTS, LANES), jnp.int32),
            pltpu.VMEM((seq_len, width), jnp.bfloat16),
            pltpu.VMEM((width, 3 * width), jnp.bfloat16),
            pltpu.VMEM((width, width), jnp.bfloat16),
            pltpu.VMEM(index_rows.shape, jnp.bfloat16),
        ],
        scratch_shapes=[
            pltpu.VMEM((room, width), jnp.bfloat16),
            pltpu.VMEM((room, 3 * width), jnp.bfloat16),
            pltpu.VMEM((room, width), jnp.bfloat16),
            pltpu.VMEM((SLOTS, width), jnp.float32),
            pltpu.SemaphoreType.DMA((6,)),
            pltpu.SemaphoreType.DMA((text_dev,)),
        ],
        compiler_params=pltpu.CompilerParams(vmem_limit_bytes=40 << 20),
        name="encode",
    )(lengths, dealing, candidates, *small, hidden, qkv_weight, out_weight, index_rows)

    def copy_sems(peers):
        return pltpu.SemaphoreType.DMA((2, peers))

    return pl.pallas_call(
        functools.partial(finish_kernel, dp_count, shard_count, text_dev),
        in_specs=[vmem] * 11,
        out_specs=vmem,
        out_shape=jax.ShapeDtypeStruct(candidates.shape, jnp.float32),
        scratch_shapes=[
            pltpu.VMEM((seq_len, 3 * width), jnp.bfloat16),
            pltpu.VMEM((seq_len, width), jnp.bfloat16),
            pltpu.VMEM((pieces, LANES), jnp.float32),
            pltpu.VMEM((shard_count, dp_count, text_dev, pieces, LANES), jnp.bfloat16),
            pltpu.VMEM((shard_count, dp_count, pieces, LANES), jnp.bfloat16),
            pltpu.VMEM((shard_count, dp_count, SLOTS, LANES), jnp.int32),
            pltpu.VMEM((compact, pieces, LANES), jnp.float32),
            pltpu.VMEM((compact, width), jnp.bfloat16),
            pltpu.VMEM((devices, pieces, LANES), jnp.float32),
            pltpu.VMEM((devices, width), jnp.bfloat16),
            pltpu.VMEM((compact, width), jnp.bfloat16),
            pltpu.VMEM((compact, compact), jnp.bfloat16),
            pltpu.VMEM((compact, devices), jnp.bfloat16),
            pltpu.VMEM((devices, PACK, LANES), jnp.float32),
            pltpu.VMEM((dp_count, shard_count, PACK, LANES), jnp.float32),
            copy_sems(dp_count),
            copy_sems(dp_count),
            copy_sems(shard_count),
            copy_sems(shard_count),
            *[pltpu.SemaphoreType.DMA((dp_count, shard_count))] * 4,
        ],
        compiler_params=pltpu.CompilerParams(
            vmem_limit_bytes=40 << 20, collective_id=0, has_side_effects=True
        ),
        name="finish",
    )(
        dealing[None, :],
        *small,
        first_queries,
        meta,
        *[
            pltpu.with_memory_space_constraint(x, pltpu.VMEM)
            for x in (long_states, qkv_held, out_held, index_held)
        ],
    )


def solution(mesh):
    in_specs = (
        P(("dp", "shard"), None, None),
        P(),
        P(),
        P(("dp", "shard"), None),
        P(("dp", "shard"), None),
        P(),
        P(),
        P(),
        P(),
        P(),
        P(),
    )
    out_specs = P(("dp", "shard"), None)
    return jax.shard_map(shards, mesh=mesh, in_specs=in_specs, out_specs=out_specs, check_vma=False)
```

```python
import functools

import jax
import jax.numpy as jnp
from jax import lax
from jax.experimental import pallas as pl
from jax.experimental.pallas import tpu as pltpu
from jax.sharding import PartitionSpec as P

HEADS = 16
HEAD = 64
LANES = 128
SLOTS = 8
GRAIN = 16
UNIT = 128
PACK = 4
ID_ROW = 6
LEN_ROW = 7


def attend(qkv_ref, context_ref, start, rows, keys_count, text_len):
    width = context_ref.shape[1]
    queries, keys = pl.ds(start, rows), pl.ds(start, keys_count)
    lane = lax.broadcasted_iota(jnp.int32, (keys_count, LANES), 1)
    place = lax.broadcasted_iota(jnp.int32, (keys_count, LANES), 0)
    first = lane < HEAD
    valid = place < text_len
    key_valid = lax.broadcasted_iota(jnp.int32, (1, keys_count), 1) < text_len
    zero = jnp.zeros((keys_count, LANES), jnp.bfloat16)
    ones = jnp.ones((keys_count, LANES), jnp.bfloat16)
    ones_a, ones_b = jnp.where(first, ones, zero), jnp.where(first, zero, ones)
    first_valid, second_valid = first & valid, jnp.logical_not(first) & valid
    logits = []
    for base in range(0, width, LANES):
        q2 = qkv_ref[queries, base : base + LANES]
        k2 = qkv_ref[keys, width + base : width + base + LANES]
        for part in (jnp.where(first, k2, zero), jnp.where(first, zero, k2)):
            logits.append(
                lax.dot_general(
                    q2, part, (((1,), (1,)), ((), ())), preferred_element_type=jnp.float32
                )
            )
    probs = []
    for part in logits:
        part = jnp.where(key_valid, part, -1e30)
        peak = jnp.max(part, axis=-1, keepdims=True)
        probs.append(jnp.exp(part - peak).astype(jnp.bfloat16))
    for pair, base in enumerate(range(0, width, LANES)):
        v2 = qkv_ref[keys, 2 * width + base : 2 * width + base + LANES]
        both = jnp.concatenate(probs[2 * pair : 2 * pair + 2], axis=1)
        values = jnp.concatenate(
            [
                jnp.concatenate([jnp.where(first_valid, v2, zero), ones_a], axis=1),
                jnp.concatenate([jnp.where(second_valid, v2, zero), ones_b], axis=1),
            ],
            axis=0,
        )
        mixed = jnp.dot(both, values, preferred_element_type=jnp.float32)
        context_ref[queries, base : base + LANES] = (mixed[:, :LANES] / mixed[:, LANES:]).astype(
            jnp.bfloat16
        )


def project(states, qkv_weight, bias_ref, qkv_ref, rows, part):
    width = states.shape[1]
    chunk = 512
    for start in range(part * width, (part + 1) * width, chunk):
        cols = slice(start, start + chunk)
        out = (
            jnp.dot(states, qkv_weight[:, cols], preferred_element_type=jnp.float32)
            + bias_ref[:, cols]
        )
        if part == 0:
            out = out * (1.0 / HEAD**0.5)
        qkv_ref[rows, cols] = out.astype(jnp.bfloat16)


def normalise(states, context, out_weight, out_bias_ref):
    resid = (
        states.astype(jnp.float32)
        + jnp.dot(context, out_weight[...], preferred_element_type=jnp.float32)
        + out_bias_ref[...]
    )
    centre = jnp.mean(resid, axis=-1, keepdims=True)
    resid = resid - centre
    spread = jnp.mean(resid * resid, axis=-1, keepdims=True)
    return resid * lax.rsqrt(spread + 1e-05)


def embed(total, count, gain_ref, shift_ref):
    pooled = total / count * gain_ref[...] + shift_ref[...]
    return pooled * lax.rsqrt(jnp.sum(pooled * pooled, axis=-1, keepdims=True) + 1e-06)


def encode_kernel(
    shard_count,
    lengths_ref,
    dealing_ref,
    cand_ref,
    qkv_bias_ref,
    out_bias_ref,
    gain_ref,
    shift_ref,
    hidden_hbm,
    qkv_weight_hbm,
    out_weight_hbm,
    index_hbm,
    queries_ref,
    meta_ref,
    long_states,
    qkv_weight,
    out_weight,
    index_rows,
    states_ref,
    qkv_ref,
    context_ref,
    fold_ref,
    load_sems,
    state_sems,
):
    text_dev, seq_len, width = hidden_hbm.shape
    me = lax.axis_index("dp") * shard_count + lax.axis_index("shard")
    texts = [dealing_ref[me * text_dev + slot] for slot in range(text_dev)]
    counts = [lengths_ref[text] for text in texts]
    ranks = []
    for slot in range(text_dev):
        rank = jnp.int32(0)
        for other in range(text_dev):
            if other < slot:
                rank = rank + jnp.where(counts[other] <= counts[slot], 1, 0)
            if other > slot:
                rank = rank + jnp.where(counts[other] < counts[slot], 1, 0)
        ranks.append(rank)

    def by_rank(values):
        out = []
        for rank in range(text_dev):
            value = values[0]
            for slot in range(1, text_dev):
                value = jnp.where(ranks[slot] == rank, values[slot], value)
            out.append(value)
        return out

    slots = by_rank(list(range(text_dev)))
    texts = by_rank(texts)
    counts = by_rank(counts)
    short_count = text_dev - long_states.shape[0] // seq_len
    starts, sizes = [], []
    total_rows = jnp.int32(0)
    for rank in range(short_count):
        size = (counts[rank] + GRAIN - 1) // GRAIN * GRAIN
        starts.append(total_rows)
        sizes.append(size)
        total_rows = total_rows + size

    def state_copy(rank):
        size = pl.multiple_of(sizes[rank], GRAIN)
        return pltpu.make_async_copy(
            hidden_hbm.at[slots[rank], pl.ds(0, size)],
            states_ref.at[pl.ds(pl.multiple_of(starts[rank], GRAIN), size)],
            state_sems.at[rank],
        )

    def long_copy(rank):
        return pltpu.make_async_copy(
            hidden_hbm.at[slots[rank]],
            long_states.at[pl.ds((rank - short_count) * seq_len, seq_len)],
            state_sems.at[rank],
        )

    loads = [
        pltpu.make_async_copy(
            qkv_weight_hbm.at[:, pl.ds(part * width, width)],
            qkv_weight.at[:, pl.ds(part * width, width)],
            load_sems.at[part],
        )
        for part in range(3)
    ]
    loads.append(pltpu.make_async_copy(out_weight_hbm, out_weight, load_sems.at[3]))
    loads += [long_copy(rank) for rank in range(short_count, text_dev)]
    loads.append(pltpu.make_async_copy(index_hbm, index_rows, load_sems.at[4]))

    for rank in range(short_count):
        state_copy(rank).start()
    for load in loads[:3]:
        load.start()
    meta_ref[...] = jnp.zeros_like(meta_ref)
    meta_ref[:text_dev, : cand_ref.shape[1]] = cand_ref[...]
    lane = lax.broadcasted_iota(jnp.int32, (1, LANES), 1)
    id_row, len_row = jnp.zeros_like(lane), jnp.zeros_like(lane)
    for rank in range(text_dev):
        id_row = jnp.where(lane == rank, texts[rank], id_row)
        len_row = jnp.where(lane == rank, counts[rank], len_row)
    meta_ref[ID_ROW : ID_ROW + 1, :] = id_row
    meta_ref[LEN_ROW : LEN_ROW + 1, :] = len_row
    for rank in range(short_count):
        state_copy(rank).wait()

    units = (total_rows + UNIT - 1) // UNIT
    full, rest = units // PACK, lax.rem(units, PACK)

    def over_rows(body):
        def step(i, carry):
            body(pl.multiple_of(i * (PACK * UNIT), PACK * UNIT), PACK * UNIT)
            return carry

        lax.fori_loop(0, full, step, 0)
        for size in range(1, PACK):
            pl.when(rest == size)(
                lambda size=size: body(
                    pl.multiple_of(full * (PACK * UNIT), PACK * UNIT), size * UNIT
                )
            )

    for part in range(3):
        loads[part].wait()
        if part == 0:
            for load in loads[3:]:
                load.start()

        def qkv_block(base, size):
            rows = pl.ds(base, size)
            project(states_ref[rows, :], qkv_weight, qkv_bias_ref, qkv_ref, rows, part)

        over_rows(qkv_block)

    def text_step(rank, carry):
        count, start = counts[0], starts[0]
        for other in range(1, short_count):
            count = jnp.where(rank == other, counts[other], count)
            start = jnp.where(rank == other, starts[other], start)
        start = pl.multiple_of(start, GRAIN)
        small = count <= 128
        large = count > 192

        @pl.when(small)
        def _():
            attend(qkv_ref, context_ref, start, 128, 128, count)

        @pl.when(jnp.logical_not(small | large))
        def _():
            attend(qkv_ref, context_ref, start, 192, 256, count)

        @pl.when(large)
        def _():
            attend(qkv_ref, context_ref, start, 256, 256, count)

        return carry

    lax.fori_loop(0, short_count, text_step, 0)

    loads[3].wait()
    slot_id = lax.broadcasted_iota(jnp.int32, (SLOTS, 1), 0)
    start_col = jnp.zeros((SLOTS, 1), jnp.int32)
    count_col = jnp.zeros((SLOTS, 1), jnp.int32)
    for rank in range(short_count):
        here = slot_id == rank
        start_col = jnp.where(here, starts[rank], start_col)
        count_col = jnp.where(here, counts[rank], count_col)
    fold_ref[...] = jnp.zeros_like(fold_ref)

    def out_block(base, size):
        rows = pl.ds(base, size)
        normed = normalise(states_ref[rows, :], context_ref[rows, :], out_weight, out_bias_ref)
        row = lax.broadcasted_iota(jnp.int32, (size, 1), 0) + base
        normed = jnp.where(row < total_rows, normed, 0.0).astype(jnp.bfloat16)
        place = lax.broadcasted_iota(jnp.int32, (SLOTS, size), 1) + base - start_col
        member = (place >= 0) & (place < count_col)
        fold_ref[...] += jnp.dot(
            jnp.where(member, 1.0, 0.0).astype(jnp.bfloat16),
            normed,
            preferred_element_type=jnp.float32,
        )

    over_rows(out_block)
    query = embed(
        fold_ref[...], jnp.maximum(count_col, 1).astype(jnp.float32), gain_ref, shift_ref
    )
    pieces = width // LANES
    for slot in range(short_count):
        for piece in range(pieces):
            queries_ref[slot, piece : piece + 1, :] = query[
                slot : slot + 1, piece * LANES : (piece + 1) * LANES
            ]
    for load in loads[4:]:
        load.wait()


def finish_kernel(
    dp_count,
    shard_count,
    qkv_bias_ref,
    out_bias_ref,
    gain_ref,
    shift_ref,
    short_queries,
    meta_ref,
    long_states,
    qkv_weight,
    out_weight,
    index_rows,
    out_ref,
    qkv_ref,
    context_ref,
    fold_ref,
    queries,
    long_queries,
    cands,
    wide_queries,
    slot_queries,
    text_queries,
    pick_ref,
    terms,
    arrived,
    dp_send,
    dp_recv,
    shard_send,
    shard_recv,
    all_send,
    all_recv,
    out_send,
    out_recv,
):
    my_dp, my_shard = lax.axis_index("dp"), lax.axis_index("shard")
    me = my_dp * shard_count + my_shard
    width = long_states.shape[1]
    short_count, pieces = short_queries.shape[:2]
    text_dev = out_ref.shape[0]
    long_count = text_dev - short_count
    seq_len = long_states.shape[0] // long_count
    devices = dp_count * shard_count
    compact = devices * text_dev

    def dp_peer(off):
        return lax.rem(my_dp + off, dp_count)

    def shard_peer(off):
        return lax.rem(my_shard + off, shard_count)

    def remote(block, send, recv, place, device):
        return pltpu.make_async_remote_copy(
            src_ref=block,
            dst_ref=block,
            send_sem=send.at[place],
            recv_sem=recv.at[place],
            device_id=device,
            device_id_type=pl.DeviceIdType.MESH,
        )

    held = [queries, cands]

    def to_dp(which, off, dp):
        block = held[which].at[my_shard, dp]
        return remote(block, dp_send, dp_recv, (which, off), (dp_peer(off), my_shard))

    def to_shard(which, off, shard):
        block = held[which].at[shard]
        return remote(block, shard_send, shard_recv, (which, off), (my_dp, shard_peer(off)))

    def dp_start(which):
        for off in range(1, dp_count):
            to_dp(which, off, my_dp).start()

    def dp_finish(which):
        for off in range(1, dp_count):
            to_dp(which, off, lax.rem(my_dp + dp_count - off, dp_count)).wait_recv()

    def shard_start(which):
        for off in range(1, shard_count):
            to_shard(which, off, my_shard).start()

    def shard_finish(which):
        for off in range(1, shard_count):
            to_shard(which, off, lax.rem(my_shard + shard_count - off, shard_count)).wait_recv()

    def sent(which):
        for off in range(1, dp_count):
            to_dp(which, off, my_dp).wait_send()
        for off in range(1, shard_count):
            to_shard(which, off, my_shard).wait_send()

    everyone = [
        (far, off)
        for far in range(dp_count)
        for off in range(shard_count)
        if (far, off) != (0, 0)
    ][::-1]

    def to_all(text, far, off, dp, shard):
        block = long_queries.at[text, shard, dp]
        return remote(
            block, all_send, all_recv, (text, far, off), (dp_peer(far), shard_peer(off))
        )

    def all_start(text):
        for far, off in everyone:
            to_all(text, far, off, my_dp, my_shard).start()

    def all_finish(text):
        for far, off in everyone:
            to_all(
                text,
                far,
                off,
                lax.rem(my_dp + dp_count - far, dp_count),
                lax.rem(my_shard + shard_count - off, shard_count),
            ).wait_recv()

    def unfold(block, rank, count):
        rows = pl.ds(rank * devices, count * devices)
        wide_queries[rows] = block.astype(jnp.float32).reshape(count * devices, pieces, LANES)
        for piece in range(pieces):
            slot_queries[rows, piece * LANES : (piece + 1) * LANES] = wide_queries[
                rows, piece, :
            ].astype(jnp.bfloat16)

    def picked(rank, count):
        rows = slice(rank * devices, (rank + count) * devices)
        return jnp.dot(
            pick_ref[:, rows], slot_queries[rows, :], preferred_element_type=jnp.float32
        )

    barrier = pltpu.get_barrier_semaphore()
    for far, off in everyone:
        pl.semaphore_signal(
            barrier,
            inc=1,
            device_id=(dp_peer(far), shard_peer(off)),
            device_id_type=pl.DeviceIdType.MESH,
        )
    queries[my_shard, my_dp] = short_queries[...].astype(jnp.bfloat16)
    cands[my_shard, my_dp] = meta_ref[...]

    states = long_states[...]
    rows = pl.ds(0, long_count * seq_len)
    project(states, qkv_weight, qkv_bias_ref, qkv_ref, rows, 0)
    pl.semaphore_wait(barrier, devices - 1)
    dp_start(0)
    dp_start(1)
    project(states, qkv_weight, qkv_bias_ref, qkv_ref, rows, 1)
    project(states, qkv_weight, qkv_bias_ref, qkv_ref, rows, 2)
    for which in (0, 1):
        dp_finish(which)
        shard_start(which)

    for text in range(long_count):
        start, rank = text * seq_len, short_count + text
        text_len = meta_ref[LEN_ROW : LEN_ROW + 1, rank : rank + 1]
        attend(qkv_ref, context_ref, start, seq_len, seq_len, text_len)
        here = pl.ds(start, seq_len)
        normed = normalise(long_states[here, :], context_ref[here, :], out_weight, out_bias_ref)
        row = lax.broadcasted_iota(jnp.int32, (seq_len, 1), 0)
        total = jnp.sum(jnp.where(row < text_len, normed, 0.0), axis=0, keepdims=True)
        query = embed(total, text_len.astype(jnp.float32), gain_ref, shift_ref)
        for piece in range(pieces):
            fold_ref[piece : piece + 1, :] = query[:, piece * LANES : (piece + 1) * LANES]
        long_queries[text, my_shard, my_dp] = fold_ref[...].astype(jnp.bfloat16)
        all_start(text)

    shard_finish(0)
    shard_finish(1)
    grouped = cands[...].reshape(devices, SLOTS, LANES)
    entry = lax.broadcasted_iota(jnp.int32, (1, compact), 1)
    block = entry % devices
    texts = ((block % dp_count) * shard_count + block // dp_count) * text_dev + entry // devices
    ids = jnp.concatenate(
        [grouped[:, ID_ROW, rank : rank + 1] for rank in range(text_dev)], axis=0
    )
    pick_ref[...] = jnp.where(ids == texts, 1.0, 0.0).T.astype(jnp.bfloat16)
    for rank in range(short_count):
        unfold(queries[:, :, rank], rank, 1)
    for text in range(long_count - 1):
        all_finish(text)
        unfold(long_queries[text], short_count + text, 1)
    first_part = picked(0, text_dev - 1)
    all_finish(long_count - 1)
    unfold(long_queries[long_count - 1], text_dev - 1, 1)
    text_queries[...] = (first_part + picked(text_dev - 1, 1)).astype(jnp.bfloat16)

    rows_here = index_rows.shape[0]
    local = (
        jnp.concatenate([grouped[:, slot, :] for slot in range(text_dev)], axis=0)
        - me * rows_here
    )
    group = local >> 7
    lane = local & (LANES - 1)
    total = jnp.zeros((compact, LANES), jnp.float32)
    rows_step = 1024
    for step in range(rows_here // rows_step):
        scores = lax.dot_general(
            text_queries[...],
            index_rows[step * rows_step : (step + 1) * rows_step, :],
            (((1,), (1,)), ((), ())),
            preferred_element_type=jnp.float32,
        )
        for part in range(rows_step // LANES):
            found = jnp.take_along_axis(
                scores[:, part * LANES : (part + 1) * LANES],
                lane,
                axis=1,
                mode="promise_in_bounds",
            )
            total = jnp.where(group == step * (rows_step // LANES) + part, found, total)

    half = text_dev // 2
    cand_count = LANES // 2
    low = lax.broadcasted_iota(jnp.int32, (half * devices, LANES), 1) < cand_count
    packed = jnp.where(
        low, total[: half * devices], pltpu.roll(total[half * devices :], cand_count, 1)
    )
    for line in range(half):
        terms[:, line, :] = packed[line * devices : (line + 1) * devices]

    def deliver(far, off):
        return pltpu.make_async_remote_copy(
            src_ref=terms.at[shard_peer(off) * dp_count + dp_peer(far)],
            dst_ref=arrived.at[far, off],
            send_sem=out_send.at[far, off],
            recv_sem=out_recv.at[far, off],
            device_id=(dp_peer(far), shard_peer(off)),
            device_id_type=pl.DeviceIdType.MESH,
        )

    for far, off in everyone:
        deliver(far, off).start()
    for which in (0, 1):
        sent(which)
    for text in range(long_count):
        for far, off in everyone:
            to_all(text, far, off, my_dp, my_shard).wait_send()
    result = terms[my_shard * dp_count + my_dp]
    for far, off in everyone:
        deliver(far, off).wait_recv()
    for far, off in everyone:
        result = result + arrived[far, off]
    out_ref[:half, :] = result[:half, :cand_count]
    out_ref[half:, :] = result[:half, cand_count:]
    for far, off in everyone:
        deliver(far, off).wait_send()


def shards(
    hidden,
    lengths,
    dealing,
    candidates,
    index_rows,
    qkv_weight,
    qkv_bias,
    out_weight,
    out_bias,
    norm_gain,
    norm_shift,
):
    text_dev, seq_len, width = hidden.shape
    dp_count, shard_count = lax.axis_size("dp"), lax.axis_size("shard")
    devices = dp_count * shard_count
    compact = devices * text_dev
    pieces = width // LANES
    hbm = pl.BlockSpec(memory_space=pl.ANY)
    vmem = pl.BlockSpec(memory_space=pltpu.VMEM)
    smem = pl.BlockSpec(memory_space=pltpu.SMEM)
    small = (qkv_bias[None, :], out_bias[None, :], norm_gain[None, :], norm_shift[None, :])
    long_count = text_dev // 2
    short_count = text_dev - long_count
    room, long_rows = short_count * seq_len, long_count * seq_len

    short_queries, meta, long_states, qkv_held, out_held, index_held = pl.pallas_call(
        functools.partial(encode_kernel, shard_count),
        in_specs=[smem, smem, *[vmem] * 5, *[hbm] * 4],
        out_specs=[vmem] * 6,
        out_shape=[
            jax.ShapeDtypeStruct((short_count, pieces, LANES), jnp.float32),
            jax.ShapeDtypeStruct((SLOTS, LANES), jnp.int32),
            pltpu.VMEM((long_rows, width), jnp.bfloat16),
            pltpu.VMEM((width, 3 * width), jnp.bfloat16),
            pltpu.VMEM((width, width), jnp.bfloat16),
            pltpu.VMEM(index_rows.shape, jnp.bfloat16),
        ],
        scratch_shapes=[
            pltpu.VMEM((room, width), jnp.bfloat16),
            pltpu.VMEM((room, 3 * width), jnp.bfloat16),
            pltpu.VMEM((room, width), jnp.bfloat16),
            pltpu.VMEM((SLOTS, width), jnp.float32),
            pltpu.SemaphoreType.DMA((5,)),
            pltpu.SemaphoreType.DMA((text_dev,)),
        ],
        compiler_params=pltpu.CompilerParams(vmem_limit_bytes=40 << 20),
        name="encode",
    )(lengths, dealing, candidates, *small, hidden, qkv_weight, out_weight, index_rows)

    def copy_sems(peers):
        return pltpu.SemaphoreType.DMA((2, peers))

    return pl.pallas_call(
        functools.partial(finish_kernel, dp_count, shard_count),
        in_specs=[vmem] * 10,
        out_specs=vmem,
        out_shape=jax.ShapeDtypeStruct(candidates.shape, jnp.float32),
        scratch_shapes=[
            pltpu.VMEM((long_rows, 3 * width), jnp.bfloat16),
            pltpu.VMEM((long_rows, width), jnp.bfloat16),
            pltpu.VMEM((pieces, LANES), jnp.float32),
            pltpu.VMEM((shard_count, dp_count, short_count, pieces, LANES), jnp.bfloat16),
            pltpu.VMEM((long_count, shard_count, dp_count, pieces, LANES), jnp.bfloat16),
            pltpu.VMEM((shard_count, dp_count, SLOTS, LANES), jnp.int32),
            pltpu.VMEM((compact, pieces, LANES), jnp.float32),
            pltpu.VMEM((compact, width), jnp.bfloat16),
            pltpu.VMEM((compact, width), jnp.bfloat16),
            pltpu.VMEM((compact, compact), jnp.bfloat16),
            pltpu.VMEM((devices, PACK, LANES), jnp.float32),
            pltpu.VMEM((dp_count, shard_count, PACK, LANES), jnp.float32),
            copy_sems(dp_count),
            copy_sems(dp_count),
            copy_sems(shard_count),
            copy_sems(shard_count),
            *[pltpu.SemaphoreType.DMA((long_count, dp_count, shard_count))] * 2,
            *[pltpu.SemaphoreType.DMA((dp_count, shard_count))] * 2,
        ],
        compiler_params=pltpu.CompilerParams(
            vmem_limit_bytes=40 << 20, collective_id=0, has_side_effects=True
        ),
        name="finish",
    )(
        *small,
        short_queries,
        meta,
        *[
            pltpu.with_memory_space_constraint(x, pltpu.VMEM)
            for x in (long_states, qkv_held, out_held, index_held)
        ],
    )


def solution(mesh):
    in_specs = (
        P(("dp", "shard"), None, None),
        P(),
        P(),
        P(("dp", "shard"), None),
        P(("dp", "shard"), None),
        P(),
        P(),
        P(),
        P(),
        P(),
        P(),
    )
    out_specs = P(("dp", "shard"), None)
    return jax.shard_map(shards, mesh=mesh, in_specs=in_specs, out_specs=out_specs, check_vma=False)
```

```python
import functools

import jax
import jax.numpy as jnp
from jax import lax
from jax.experimental import pallas as pl
from jax.experimental.pallas import tpu as pltpu
from jax.sharding import PartitionSpec as P

HEADS = 16
HEAD = 64
LANES = 128
SLOTS = 8
GRAIN = 16
UNIT = 128
PACK = 4
ID_ROW = 6
LEN_ROW = 7


def attend(qkv_ref, context_ref, start, rows, keys_count, text_len):
    width = context_ref.shape[1]
    queries, keys = pl.ds(start, rows), pl.ds(start, keys_count)
    lane = lax.broadcasted_iota(jnp.int32, (keys_count, LANES), 1)
    place = lax.broadcasted_iota(jnp.int32, (keys_count, LANES), 0)
    first = lane < HEAD
    valid = place < text_len
    key_valid = lax.broadcasted_iota(jnp.int32, (1, keys_count), 1) < text_len
    zero = jnp.zeros((keys_count, LANES), jnp.bfloat16)
    ones = jnp.ones((keys_count, LANES), jnp.bfloat16)
    ones_a, ones_b = jnp.where(first, ones, zero), jnp.where(first, zero, ones)
    first_valid, second_valid = first & valid, jnp.logical_not(first) & valid
    logits = []
    for base in range(0, width, LANES):
        q2 = qkv_ref[queries, base : base + LANES]
        k2 = qkv_ref[keys, width + base : width + base + LANES]
        for part in (jnp.where(first, k2, zero), jnp.where(first, zero, k2)):
            logits.append(
                lax.dot_general(
                    q2, part, (((1,), (1,)), ((), ())), preferred_element_type=jnp.float32
                )
            )
    probs = []
    for part in logits:
        part = jnp.where(key_valid, part, -1e30)
        peak = jnp.max(part, axis=-1, keepdims=True)
        probs.append(jnp.exp(part - peak).astype(jnp.bfloat16))
    for pair, base in enumerate(range(0, width, LANES)):
        v2 = qkv_ref[keys, 2 * width + base : 2 * width + base + LANES]
        both = jnp.concatenate(probs[2 * pair : 2 * pair + 2], axis=1)
        values = jnp.concatenate(
            [
                jnp.concatenate([jnp.where(first_valid, v2, zero), ones_a], axis=1),
                jnp.concatenate([jnp.where(second_valid, v2, zero), ones_b], axis=1),
            ],
            axis=0,
        )
        mixed = jnp.dot(both, values, preferred_element_type=jnp.float32)
        context_ref[queries, base : base + LANES] = (mixed[:, :LANES] / mixed[:, LANES:]).astype(
            jnp.bfloat16
        )


def project(states, qkv_weight, bias_ref, qkv_ref, rows, part):
    width = states.shape[1]
    chunk = 512
    for start in range(part * width, (part + 1) * width, chunk):
        cols = slice(start, start + chunk)
        out = (
            jnp.dot(states, qkv_weight[:, cols], preferred_element_type=jnp.float32)
            + bias_ref[:, cols]
        )
        if part == 0:
            out = out * (1.0 / HEAD**0.5)
        qkv_ref[rows, cols] = out.astype(jnp.bfloat16)


def normalise(states, context, out_weight, out_bias_ref):
    resid = (
        states.astype(jnp.float32)
        + jnp.dot(context, out_weight[...], preferred_element_type=jnp.float32)
        + out_bias_ref[...]
    )
    centre = jnp.mean(resid, axis=-1, keepdims=True)
    resid = resid - centre
    spread = jnp.mean(resid * resid, axis=-1, keepdims=True)
    return resid * lax.rsqrt(spread + 1e-05)


def embed(total, count, gain_ref, shift_ref):
    pooled = total / count * gain_ref[...] + shift_ref[...]
    return pooled * lax.rsqrt(jnp.sum(pooled * pooled, axis=-1, keepdims=True) + 1e-06)


def encode_kernel(
    shard_count,
    lengths_ref,
    dealing_ref,
    cand_ref,
    qkv_bias_ref,
    out_bias_ref,
    gain_ref,
    shift_ref,
    hidden_hbm,
    qkv_weight_hbm,
    out_weight_hbm,
    index_hbm,
    queries_ref,
    meta_ref,
    long_states,
    qkv_weight,
    out_weight,
    index_rows,
    states_ref,
    qkv_ref,
    context_ref,
    fold_ref,
    load_sems,
    state_sems,
):
    text_dev, seq_len, width = hidden_hbm.shape
    loads = [
        pltpu.make_async_copy(
            qkv_weight_hbm.at[:, pl.ds(part * width, width)],
            qkv_weight.at[:, pl.ds(part * width, width)],
            load_sems.at[part],
        )
        for part in range(3)
    ]
    for load in loads:
        load.start()
    me = lax.axis_index("dp") * shard_count + lax.axis_index("shard")
    texts = [dealing_ref[me * text_dev + slot] for slot in range(text_dev)]
    counts = [lengths_ref[text] for text in texts]
    ranks = []
    for slot in range(text_dev):
        rank = jnp.int32(0)
        for other in range(text_dev):
            if other < slot:
                rank = rank + jnp.where(counts[other] <= counts[slot], 1, 0)
            if other > slot:
                rank = rank + jnp.where(counts[other] < counts[slot], 1, 0)
        ranks.append(rank)

    def by_rank(values):
        out = []
        for rank in range(text_dev):
            value = values[0]
            for slot in range(1, text_dev):
                value = jnp.where(ranks[slot] == rank, values[slot], value)
            out.append(value)
        return out

    slots = by_rank(list(range(text_dev)))
    texts = by_rank(texts)
    counts = by_rank(counts)
    short_count = text_dev - long_states.shape[0] // seq_len
    starts, sizes = [], []
    total_rows = jnp.int32(0)
    for rank in range(short_count):
        size = (counts[rank] + GRAIN - 1) // GRAIN * GRAIN
        starts.append(total_rows)
        sizes.append(size)
        total_rows = total_rows + size

    def state_copy(rank):
        size = pl.multiple_of(sizes[rank], GRAIN)
        return pltpu.make_async_copy(
            hidden_hbm.at[slots[rank], pl.ds(0, size)],
            states_ref.at[pl.ds(pl.multiple_of(starts[rank], GRAIN), size)],
            state_sems.at[rank],
        )

    def long_copy(rank):
        return pltpu.make_async_copy(
            hidden_hbm.at[slots[rank]],
            long_states.at[pl.ds((rank - short_count) * seq_len, seq_len)],
            state_sems.at[rank],
        )

    loads.append(pltpu.make_async_copy(out_weight_hbm, out_weight, load_sems.at[3]))
    loads += [long_copy(rank) for rank in range(short_count, text_dev)]
    loads.append(pltpu.make_async_copy(index_hbm, index_rows, load_sems.at[4]))

    for rank in range(short_count):
        state_copy(rank).start()
    meta_ref[...] = jnp.zeros_like(meta_ref)
    meta_ref[:text_dev, : cand_ref.shape[1]] = cand_ref[...]
    lane = lax.broadcasted_iota(jnp.int32, (1, LANES), 1)
    id_row, len_row = jnp.zeros_like(lane), jnp.zeros_like(lane)
    for rank in range(text_dev):
        id_row = jnp.where(lane == rank, texts[rank], id_row)
        len_row = jnp.where(lane == rank, counts[rank], len_row)
    meta_ref[ID_ROW : ID_ROW + 1, :] = id_row
    meta_ref[LEN_ROW : LEN_ROW + 1, :] = len_row
    for rank in range(short_count):
        state_copy(rank).wait()

    units = (total_rows + UNIT - 1) // UNIT
    full, rest = units // PACK, lax.rem(units, PACK)

    def over_rows(body):
        def step(i, carry):
            body(pl.multiple_of(i * (PACK * UNIT), PACK * UNIT), PACK * UNIT)
            return carry

        lax.fori_loop(0, full, step, 0)
        for size in range(1, PACK):
            pl.when(rest == size)(
                lambda size=size: body(
                    pl.multiple_of(full * (PACK * UNIT), PACK * UNIT), size * UNIT
                )
            )

    for part in range(3):
        loads[part].wait()
        if part == 0:
            for load in loads[3:]:
                load.start()

        def qkv_block(base, size):
            rows = pl.ds(base, size)
            project(states_ref[rows, :], qkv_weight, qkv_bias_ref, qkv_ref, rows, part)

        over_rows(qkv_block)

    def text_step(rank, carry):
        count, start = counts[0], starts[0]
        for other in range(1, short_count):
            count = jnp.where(rank == other, counts[other], count)
            start = jnp.where(rank == other, starts[other], start)
        start = pl.multiple_of(start, GRAIN)
        small = count <= 128
        large = count > 192

        @pl.when(small)
        def _():
            attend(qkv_ref, context_ref, start, 128, 128, count)

        @pl.when(jnp.logical_not(small | large))
        def _():
            attend(qkv_ref, context_ref, start, 192, 256, count)

        @pl.when(large)
        def _():
            attend(qkv_ref, context_ref, start, 256, 256, count)

        return carry

    lax.fori_loop(0, short_count, text_step, 0)

    loads[3].wait()
    slot_id = lax.broadcasted_iota(jnp.int32, (SLOTS, 1), 0)
    start_col = jnp.zeros((SLOTS, 1), jnp.int32)
    count_col = jnp.zeros((SLOTS, 1), jnp.int32)
    for rank in range(short_count):
        here = slot_id == rank
        start_col = jnp.where(here, starts[rank], start_col)
        count_col = jnp.where(here, counts[rank], count_col)
    fold_ref[...] = jnp.zeros_like(fold_ref)

    def out_block(base, size):
        rows = pl.ds(base, size)
        normed = normalise(states_ref[rows, :], context_ref[rows, :], out_weight, out_bias_ref)
        row = lax.broadcasted_iota(jnp.int32, (size, 1), 0) + base
        normed = jnp.where(row < total_rows, normed, 0.0).astype(jnp.bfloat16)
        place = lax.broadcasted_iota(jnp.int32, (SLOTS, size), 1) + base - start_col
        member = (place >= 0) & (place < count_col)
        fold_ref[...] += jnp.dot(
            jnp.where(member, 1.0, 0.0).astype(jnp.bfloat16),
            normed,
            preferred_element_type=jnp.float32,
        )

    over_rows(out_block)
    query = embed(
        fold_ref[...], jnp.maximum(count_col, 1).astype(jnp.float32), gain_ref, shift_ref
    )
    pieces = width // LANES
    for slot in range(short_count):
        for piece in range(pieces):
            queries_ref[slot, piece : piece + 1, :] = query[
                slot : slot + 1, piece * LANES : (piece + 1) * LANES
            ]
    for load in loads[4:]:
        load.wait()


def finish_kernel(
    dp_count,
    shard_count,
    qkv_bias_ref,
    out_bias_ref,
    gain_ref,
    shift_ref,
    short_queries,
    meta_ref,
    long_states,
    qkv_weight,
    out_weight,
    index_rows,
    out_ref,
    qkv_ref,
    context_ref,
    fold_ref,
    queries,
    long_queries,
    cands,
    wide_queries,
    slot_queries,
    text_queries,
    pick_ref,
    terms,
    arrived,
    dp_send,
    dp_recv,
    shard_send,
    shard_recv,
    all_send,
    all_recv,
    out_send,
    out_recv,
):
    my_dp, my_shard = lax.axis_index("dp"), lax.axis_index("shard")
    me = my_dp * shard_count + my_shard
    width = long_states.shape[1]
    short_count, pieces = short_queries.shape[:2]
    text_dev = out_ref.shape[0]
    long_count = text_dev - short_count
    seq_len = long_states.shape[0] // long_count
    devices = dp_count * shard_count
    compact = devices * text_dev

    def dp_peer(off):
        return lax.rem(my_dp + off, dp_count)

    def shard_peer(off):
        return lax.rem(my_shard + off, shard_count)

    def remote(block, send, recv, device):
        return pltpu.make_async_remote_copy(
            src_ref=block,
            dst_ref=block,
            send_sem=send,
            recv_sem=recv,
            device_id=device,
            device_id_type=pl.DeviceIdType.MESH,
        )

    held = [queries, cands]

    def settle(blocks, sem):
        pltpu.make_async_copy(blocks, blocks, sem).wait()

    def dp_start(which):
        block = held[which].at[my_shard, my_dp]
        for off in range(1, dp_count):
            place = (dp_peer(off), my_shard)
            remote(block, dp_send.at[which], dp_recv.at[which], place).start()

    def dp_settle(which, sems):
        settle(held[which].at[0, pl.ds(0, dp_count - 1)], sems.at[which])

    def shard_start(which):
        block = held[which].at[my_shard]
        for off in range(1, shard_count):
            place = (my_dp, shard_peer(off))
            remote(block, shard_send.at[which], shard_recv.at[which], place).start()

    def shard_settle(which, sems):
        settle(held[which].at[pl.ds(0, shard_count - 1)], sems.at[which])

    everyone = [
        (far, off)
        for far in range(dp_count)
        for off in range(shard_count)
        if (far, off) != (0, 0)
    ][::-1]
    mine = my_shard * dp_count + my_dp

    def all_start(text):
        block = long_queries.at[text, mine]
        for far, off in everyone:
            place = (dp_peer(far), shard_peer(off))
            remote(block, all_send.at[text], all_recv.at[text], place).start()

    def all_settle(text, sems):
        settle(long_queries.at[text, pl.ds(0, devices - 1)], sems.at[text])

    def unfold(block, rank, count):
        rows = pl.ds(rank * devices, count * devices)
        wide_queries[rows] = block.astype(jnp.float32).reshape(count * devices, pieces, LANES)
        for piece in range(pieces):
            slot_queries[rows, piece * LANES : (piece + 1) * LANES] = wide_queries[
                rows, piece, :
            ].astype(jnp.bfloat16)

    def picked(rank, count):
        rows = slice(rank * devices, (rank + count) * devices)
        return jnp.dot(
            pick_ref[:, rows], slot_queries[rows, :], preferred_element_type=jnp.float32
        )

    barrier = pltpu.get_barrier_semaphore()
    for far, off in everyone:
        pl.semaphore_signal(
            barrier,
            inc=1,
            device_id=(dp_peer(far), shard_peer(off)),
            device_id_type=pl.DeviceIdType.MESH,
        )
    queries[my_shard, my_dp] = short_queries[...].astype(jnp.bfloat16)
    cands[my_shard, my_dp] = meta_ref[...]

    states = long_states[...]
    rows = pl.ds(0, long_count * seq_len)
    pl.semaphore_wait(barrier, devices - 1)
    dp_start(0)
    dp_start(1)
    project(states, qkv_weight, qkv_bias_ref, qkv_ref, rows, 0)
    project(states, qkv_weight, qkv_bias_ref, qkv_ref, rows, 1)
    project(states, qkv_weight, qkv_bias_ref, qkv_ref, rows, 2)
    for which in (0, 1):
        dp_settle(which, dp_recv)
        shard_start(which)

    for text in range(long_count):
        start, rank = text * seq_len, short_count + text
        text_len = meta_ref[LEN_ROW : LEN_ROW + 1, rank : rank + 1]
        attend(qkv_ref, context_ref, start, seq_len, seq_len, text_len)
        here = pl.ds(start, seq_len)
        normed = normalise(long_states[here, :], context_ref[here, :], out_weight, out_bias_ref)
        row = lax.broadcasted_iota(jnp.int32, (seq_len, 1), 0)
        total = jnp.sum(jnp.where(row < text_len, normed, 0.0), axis=0, keepdims=True)
        query = embed(total, text_len.astype(jnp.float32), gain_ref, shift_ref)
        for piece in range(pieces):
            fold_ref[piece : piece + 1, :] = query[:, piece * LANES : (piece + 1) * LANES]
        long_queries[text, mine] = fold_ref[...].astype(jnp.bfloat16)
        all_start(text)

    shard_settle(0, shard_recv)
    shard_settle(1, shard_recv)
    grouped = cands[...].reshape(devices, SLOTS, LANES)
    entry = lax.broadcasted_iota(jnp.int32, (1, compact), 1)
    block = entry % devices
    texts = ((block % dp_count) * shard_count + block // dp_count) * text_dev + entry // devices
    ids = jnp.concatenate(
        [grouped[:, ID_ROW, rank : rank + 1] for rank in range(text_dev)], axis=0
    )
    pick_ref[...] = jnp.where(ids == texts, 1.0, 0.0).T.astype(jnp.bfloat16)
    for rank in range(short_count):
        unfold(queries[:, :, rank], rank, 1)
    for text in range(long_count - 1):
        all_settle(text, all_recv)
        unfold(long_queries[text], short_count + text, 1)
    first_part = picked(0, text_dev - 1)
    all_settle(long_count - 1, all_recv)
    unfold(long_queries[long_count - 1], text_dev - 1, 1)
    text_queries[...] = (first_part + picked(text_dev - 1, 1)).astype(jnp.bfloat16)

    rows_here = index_rows.shape[0]
    local = (
        jnp.concatenate([grouped[:, slot, :] for slot in range(text_dev)], axis=0)
        - me * rows_here
    )
    group = local >> 7
    lane = local & (LANES - 1)
    total = jnp.zeros((compact, LANES), jnp.float32)
    rows_step = 1024
    for step in range(rows_here // rows_step):
        scores = lax.dot_general(
            text_queries[...],
            index_rows[step * rows_step : (step + 1) * rows_step, :],
            (((1,), (1,)), ((), ())),
            preferred_element_type=jnp.float32,
        )
        for part in range(rows_step // LANES):
            found = jnp.take_along_axis(
                scores[:, part * LANES : (part + 1) * LANES],
                lane,
                axis=1,
                mode="promise_in_bounds",
            )
            total = jnp.where(group == step * (rows_step // LANES) + part, found, total)

    half = text_dev // 2
    cand_count = LANES // 2
    low = lax.broadcasted_iota(jnp.int32, (half * devices, LANES), 1) < cand_count
    packed = jnp.where(
        low, total[: half * devices], pltpu.roll(total[half * devices :], cand_count, 1)
    )
    for line in range(half):
        terms[:, line, :] = packed[line * devices : (line + 1) * devices]

    for far, off in everyone:
        pltpu.make_async_remote_copy(
            src_ref=terms.at[shard_peer(off) * dp_count + dp_peer(far)],
            dst_ref=arrived.at[far * shard_count + off],
            send_sem=out_send,
            recv_sem=out_recv,
            device_id=(dp_peer(far), shard_peer(off)),
            device_id_type=pl.DeviceIdType.MESH,
        ).start()
    for which in (0, 1):
        dp_settle(which, dp_send)
        shard_settle(which, shard_send)
    for text in range(long_count):
        all_settle(text, all_send)
    others = arrived.at[pl.ds(1, devices - 1)]
    settle(others, out_recv)
    result = terms[mine] + jnp.sum(others[...], axis=0)
    out_ref[:half, :] = result[:half, :cand_count]
    out_ref[half:, :] = result[:half, cand_count:]
    settle(others, out_send)


def shards(
    hidden,
    lengths,
    dealing,
    candidates,
    index_rows,
    qkv_weight,
    qkv_bias,
    out_weight,
    out_bias,
    norm_gain,
    norm_shift,
):
    text_dev, seq_len, width = hidden.shape
    dp_count, shard_count = lax.axis_size("dp"), lax.axis_size("shard")
    devices = dp_count * shard_count
    compact = devices * text_dev
    pieces = width // LANES
    hbm = pl.BlockSpec(memory_space=pl.ANY)
    vmem = pl.BlockSpec(memory_space=pltpu.VMEM)
    smem = pl.BlockSpec(memory_space=pltpu.SMEM)
    small = (qkv_bias[None, :], out_bias[None, :], norm_gain[None, :], norm_shift[None, :])
    long_count = text_dev // 3
    short_count = text_dev - long_count
    room, long_rows = short_count * seq_len, long_count * seq_len

    short_queries, meta, long_states, qkv_held, out_held, index_held = pl.pallas_call(
        functools.partial(encode_kernel, shard_count),
        in_specs=[smem, smem, *[vmem] * 5, *[hbm] * 4],
        out_specs=[vmem] * 6,
        out_shape=[
            jax.ShapeDtypeStruct((short_count, pieces, LANES), jnp.float32),
            jax.ShapeDtypeStruct((SLOTS, LANES), jnp.int32),
            pltpu.VMEM((long_rows, width), jnp.bfloat16),
            pltpu.VMEM((width, 3 * width), jnp.bfloat16),
            pltpu.VMEM((width, width), jnp.bfloat16),
            pltpu.VMEM(index_rows.shape, jnp.bfloat16),
        ],
        scratch_shapes=[
            pltpu.VMEM((room, width), jnp.bfloat16),
            pltpu.VMEM((room, 3 * width), jnp.bfloat16),
            pltpu.VMEM((room, width), jnp.bfloat16),
            pltpu.VMEM((SLOTS, width), jnp.float32),
            pltpu.SemaphoreType.DMA((5,)),
            pltpu.SemaphoreType.DMA((text_dev,)),
        ],
        compiler_params=pltpu.CompilerParams(vmem_limit_bytes=40 << 20),
        name="encode",
    )(lengths, dealing, candidates, *small, hidden, qkv_weight, out_weight, index_rows)

    return pl.pallas_call(
        functools.partial(finish_kernel, dp_count, shard_count),
        in_specs=[vmem] * 10,
        out_specs=vmem,
        out_shape=jax.ShapeDtypeStruct(candidates.shape, jnp.float32),
        scratch_shapes=[
            pltpu.VMEM((long_rows, 3 * width), jnp.bfloat16),
            pltpu.VMEM((long_rows, width), jnp.bfloat16),
            pltpu.VMEM((pieces, LANES), jnp.float32),
            pltpu.VMEM((shard_count, dp_count, short_count, pieces, LANES), jnp.bfloat16),
            pltpu.VMEM((long_count, devices, pieces, LANES), jnp.bfloat16),
            pltpu.VMEM((shard_count, dp_count, SLOTS, LANES), jnp.int32),
            pltpu.VMEM((compact, pieces, LANES), jnp.float32),
            pltpu.VMEM((compact, width), jnp.bfloat16),
            pltpu.VMEM((compact, width), jnp.bfloat16),
            pltpu.VMEM((compact, compact), jnp.bfloat16),
            pltpu.VMEM((devices, PACK, LANES), jnp.float32),
            pltpu.VMEM((devices, PACK, LANES), jnp.float32),
            *[pltpu.SemaphoreType.DMA((2,))] * 4,
            *[pltpu.SemaphoreType.DMA((long_count,))] * 2,
            *[pltpu.SemaphoreType.DMA] * 2,
        ],
        compiler_params=pltpu.CompilerParams(
            vmem_limit_bytes=40 << 20, collective_id=0, has_side_effects=True
        ),
        name="finish",
    )(
        *small,
        short_queries,
        meta,
        *[
            pltpu.with_memory_space_constraint(x, pltpu.VMEM)
            for x in (long_states, qkv_held, out_held, index_held)
        ],
    )


def solution(mesh):
    in_specs = (
        P(("dp", "shard"), None, None),
        P(),
        P(),
        P(("dp", "shard"), None),
        P(("dp", "shard"), None),
        P(),
        P(),
        P(),
        P(),
        P(),
        P(),
    )
    out_specs = P(("dp", "shard"), None)
    return jax.shard_map(shards, mesh=mesh, in_specs=in_specs, out_specs=out_specs, check_vma=False)
```

```python
import functools

import jax
import jax.numpy as jnp
from jax import lax
from jax.experimental import pallas as pl
from jax.experimental.pallas import tpu as pltpu
from jax.sharding import PartitionSpec as P

HEADS = 16
HEAD = 64
LANES = 128
SLOTS = 8
GRAIN = 16
UNIT = 128
PACK = 4
LEN_LANE = 64


def attend(qkv_ref, context_ref, start, rows, keys_count, text_len):
    width = context_ref.shape[1]
    queries, keys = pl.ds(start, rows), pl.ds(start, keys_count)
    lane = lax.broadcasted_iota(jnp.int32, (keys_count, LANES), 1)
    place = lax.broadcasted_iota(jnp.int32, (keys_count, LANES), 0)
    first = lane < HEAD
    valid = place < text_len
    key_valid = lax.broadcasted_iota(jnp.int32, (1, keys_count), 1) < text_len
    zero = jnp.zeros((keys_count, LANES), jnp.bfloat16)
    ones = jnp.ones((keys_count, LANES), jnp.bfloat16)
    ones_a, ones_b = jnp.where(first, ones, zero), jnp.where(first, zero, ones)
    first_valid, second_valid = first & valid, jnp.logical_not(first) & valid
    logits = []
    for base in range(0, width, LANES):
        q2 = qkv_ref[queries, base : base + LANES]
        k2 = qkv_ref[keys, width + base : width + base + LANES]
        for part in (jnp.where(first, k2, zero), jnp.where(first, zero, k2)):
            logits.append(
                lax.dot_general(
                    q2, part, (((1,), (1,)), ((), ())), preferred_element_type=jnp.float32
                )
            )
    probs = []
    for part in logits:
        part = jnp.where(key_valid, part, -1e30)
        peak = jnp.max(part, axis=-1, keepdims=True)
        probs.append(jnp.exp(part - peak).astype(jnp.bfloat16))
    for pair, base in enumerate(range(0, width, LANES)):
        v2 = qkv_ref[keys, 2 * width + base : 2 * width + base + LANES]
        both = jnp.concatenate(probs[2 * pair : 2 * pair + 2], axis=1)
        values = jnp.concatenate(
            [
                jnp.concatenate([jnp.where(first_valid, v2, zero), ones_a], axis=1),
                jnp.concatenate([jnp.where(second_valid, v2, zero), ones_b], axis=1),
            ],
            axis=0,
        )
        mixed = jnp.dot(both, values, preferred_element_type=jnp.float32)
        context_ref[queries, base : base + LANES] = (mixed[:, :LANES] / mixed[:, LANES:]).astype(
            jnp.bfloat16
        )


def project(states, qkv_weight, bias_ref, qkv_ref, rows, part):
    width = states.shape[1]
    chunk = 512
    for start in range(part * width, (part + 1) * width, chunk):
        cols = slice(start, start + chunk)
        out = (
            jnp.dot(states, qkv_weight[:, cols], preferred_element_type=jnp.float32)
            + bias_ref[:, cols]
        )
        if part == 0:
            out = out * (1.0 / HEAD**0.5)
        qkv_ref[rows, cols] = out.astype(jnp.bfloat16)


def normalise(states, context, out_weight, out_bias_ref):
    resid = (
        states.astype(jnp.float32)
        + jnp.dot(context, out_weight[...], preferred_element_type=jnp.float32)
        + out_bias_ref[...]
    )
    centre = jnp.mean(resid, axis=-1, keepdims=True)
    resid = resid - centre
    spread = jnp.mean(resid * resid, axis=-1, keepdims=True)
    return resid * lax.rsqrt(spread + 1e-05)


def embed(total, count, gain_ref, shift_ref):
    pooled = total / count * gain_ref[...] + shift_ref[...]
    return pooled * lax.rsqrt(jnp.sum(pooled * pooled, axis=-1, keepdims=True) + 1e-06)


def encode_kernel(
    shard_count,
    lengths_hbm,
    dealing_hbm,
    cand_hbm,
    qkv_bias_hbm,
    out_bias_hbm,
    gain_hbm,
    shift_hbm,
    hidden_hbm,
    qkv_weight_hbm,
    out_weight_hbm,
    index_hbm,
    queries_ref,
    meta_ref,
    qkv_bias_ref,
    out_bias_ref,
    gain_ref,
    shift_ref,
    long_states,
    qkv_weight,
    out_weight,
    index_rows,
    states_ref,
    qkv_ref,
    context_ref,
    fold_ref,
    lengths_ref,
    dealing_ref,
    cand_ref,
    load_sems,
    state_sems,
    small_sems,
):
    text_dev, seq_len, width = hidden_hbm.shape
    loads = [
        pltpu.make_async_copy(
            qkv_weight_hbm.at[:, pl.ds(part * width, width)],
            qkv_weight.at[:, pl.ds(part * width, width)],
            load_sems.at[part],
        )
        for part in range(3)
    ]
    smalls = [
        pltpu.make_async_copy(source, target, small_sems.at[place])
        for place, (source, target) in enumerate(
            [
                (lengths_hbm, lengths_ref),
                (dealing_hbm, dealing_ref),
                (cand_hbm, cand_ref),
                (qkv_bias_hbm, qkv_bias_ref),
                (out_bias_hbm, out_bias_ref),
                (gain_hbm, gain_ref),
                (shift_hbm, shift_ref),
            ]
        )
    ]
    for small in smalls:
        small.start()
    for load in loads:
        load.start()
    for small in smalls[:2]:
        small.wait()
    me = lax.axis_index("dp") * shard_count + lax.axis_index("shard")
    texts = [dealing_ref[me * text_dev + slot] for slot in range(text_dev)]
    counts = [lengths_ref[text] for text in texts]
    ranks = []
    for slot in range(text_dev):
        rank = jnp.int32(0)
        for other in range(text_dev):
            if other < slot:
                rank = rank + jnp.where(counts[other] <= counts[slot], 1, 0)
            if other > slot:
                rank = rank + jnp.where(counts[other] < counts[slot], 1, 0)
        ranks.append(rank)

    def by_rank(values):
        out = []
        for rank in range(text_dev):
            value = values[0]
            for slot in range(1, text_dev):
                value = jnp.where(ranks[slot] == rank, values[slot], value)
            out.append(value)
        return out

    slots = by_rank(list(range(text_dev)))
    texts = by_rank(texts)
    counts = by_rank(counts)
    short_count = text_dev - long_states.shape[0] // seq_len
    starts, sizes = [], []
    total_rows = jnp.int32(0)
    for rank in range(short_count):
        size = (counts[rank] + GRAIN - 1) // GRAIN * GRAIN
        starts.append(total_rows)
        sizes.append(size)
        total_rows = total_rows + size

    def state_copy(rank):
        size = pl.multiple_of(sizes[rank], GRAIN)
        return pltpu.make_async_copy(
            hidden_hbm.at[slots[rank], pl.ds(0, size)],
            states_ref.at[pl.ds(pl.multiple_of(starts[rank], GRAIN), size)],
            state_sems.at[rank],
        )

    def long_copy(rank):
        return pltpu.make_async_copy(
            hidden_hbm.at[slots[rank]],
            long_states.at[pl.ds((rank - short_count) * seq_len, seq_len)],
            state_sems.at[rank],
        )

    loads.append(pltpu.make_async_copy(out_weight_hbm, out_weight, load_sems.at[3]))
    loads += [long_copy(rank) for rank in range(short_count, text_dev)]
    loads.append(pltpu.make_async_copy(index_hbm, index_rows, load_sems.at[4]))

    for rank in range(short_count):
        state_copy(rank).start()
    for small in smalls[2:]:
        small.wait()
    half = text_dev // 2
    meta_ref[:half, :] = jnp.concatenate([cand_ref[:half, :], cand_ref[half:, :]], axis=1)
    lane = lax.broadcasted_iota(jnp.int32, (1, LANES), 1)
    row = jnp.zeros_like(lane)
    for rank in range(text_dev):
        row = jnp.where(lane == rank, texts[rank], row)
        row = jnp.where(lane == LEN_LANE + rank, counts[rank], row)
    meta_ref[half:, :] = row
    for rank in range(short_count):
        state_copy(rank).wait()

    units = (total_rows + UNIT - 1) // UNIT
    full, rest = units // PACK, lax.rem(units, PACK)

    def over_rows(body):
        def step(i, carry):
            body(pl.multiple_of(i * (PACK * UNIT), PACK * UNIT), PACK * UNIT)
            return carry

        lax.fori_loop(0, full, step, 0)
        for size in range(1, PACK):
            pl.when(rest == size)(
                lambda size=size: body(
                    pl.multiple_of(full * (PACK * UNIT), PACK * UNIT), size * UNIT
                )
            )

    for part in range(3):
        loads[part].wait()
        if part == 2:
            for load in loads[3:]:
                load.start()

        def qkv_block(base, size):
            rows = pl.ds(base, size)
            project(states_ref[rows, :], qkv_weight, qkv_bias_ref, qkv_ref, rows, part)

        over_rows(qkv_block)

    def text_step(rank, carry):
        count, start = counts[0], starts[0]
        for other in range(1, short_count):
            count = jnp.where(rank == other, counts[other], count)
            start = jnp.where(rank == other, starts[other], start)
        start = pl.multiple_of(start, GRAIN)
        small = count <= 128
        large = count > 192

        @pl.when(small)
        def _():
            attend(qkv_ref, context_ref, start, 128, 128, count)

        @pl.when(jnp.logical_not(small | large))
        def _():
            attend(qkv_ref, context_ref, start, 192, 256, count)

        @pl.when(large)
        def _():
            attend(qkv_ref, context_ref, start, 256, 256, count)

        return carry

    lax.fori_loop(0, short_count, text_step, 0)

    loads[3].wait()
    slot_id = lax.broadcasted_iota(jnp.int32, (SLOTS, 1), 0)
    start_col = jnp.zeros((SLOTS, 1), jnp.int32)
    count_col = jnp.zeros((SLOTS, 1), jnp.int32)
    for rank in range(short_count):
        here = slot_id == rank
        start_col = jnp.where(here, starts[rank], start_col)
        count_col = jnp.where(here, counts[rank], count_col)
    fold_ref[...] = jnp.zeros_like(fold_ref)

    def out_block(base, size):
        rows = pl.ds(base, size)
        normed = normalise(states_ref[rows, :], context_ref[rows, :], out_weight, out_bias_ref)
        row = lax.broadcasted_iota(jnp.int32, (size, 1), 0) + base
        normed = jnp.where(row < total_rows, normed, 0.0).astype(jnp.bfloat16)
        place = lax.broadcasted_iota(jnp.int32, (SLOTS, size), 1) + base - start_col
        member = (place >= 0) & (place < count_col)
        fold_ref[...] += jnp.dot(
            jnp.where(member, 1.0, 0.0).astype(jnp.bfloat16),
            normed,
            preferred_element_type=jnp.float32,
        )

    over_rows(out_block)
    query = embed(
        fold_ref[...], jnp.maximum(count_col, 1).astype(jnp.float32), gain_ref, shift_ref
    )
    pieces = width // LANES
    for slot in range(short_count):
        for piece in range(pieces):
            queries_ref[slot, piece : piece + 1, :] = query[
                slot : slot + 1, piece * LANES : (piece + 1) * LANES
            ]
    for load in loads[4:]:
        load.wait()


def finish_kernel(
    dp_count,
    shard_count,
    short_queries,
    meta_ref,
    qkv_bias_ref,
    out_bias_ref,
    gain_ref,
    shift_ref,
    long_states,
    qkv_weight,
    out_weight,
    index_rows,
    out_ref,
    qkv_ref,
    context_ref,
    fold_ref,
    queries,
    long_queries,
    cands,
    wide_queries,
    slot_queries,
    text_queries,
    pick_ref,
    terms,
    arrived,
    dp_send,
    dp_recv,
    shard_send,
    shard_recv,
    all_send,
    all_recv,
    out_send,
    out_recv,
):
    my_dp, my_shard = lax.axis_index("dp"), lax.axis_index("shard")
    me = my_dp * shard_count + my_shard
    width = long_states.shape[1]
    short_count, pieces = short_queries.shape[:2]
    text_dev = out_ref.shape[0]
    long_count = text_dev - short_count
    seq_len = long_states.shape[0] // long_count
    devices = dp_count * shard_count
    compact = devices * text_dev
    half = text_dev // 2

    def dp_peer(off):
        return lax.rem(my_dp + off, dp_count)

    def shard_peer(off):
        return lax.rem(my_shard + off, shard_count)

    def remote(block, send, recv, device):
        return pltpu.make_async_remote_copy(
            src_ref=block,
            dst_ref=block,
            send_sem=send,
            recv_sem=recv,
            device_id=device,
            device_id_type=pl.DeviceIdType.MESH,
        )

    held = [queries, cands]

    def settle(blocks, sem):
        pltpu.make_async_copy(blocks, blocks, sem).wait()

    def dp_start(which):
        block = held[which].at[my_shard, my_dp]
        for off in range(1, dp_count):
            place = (dp_peer(off), my_shard)
            remote(block, dp_send.at[which], dp_recv.at[which], place).start()

    def dp_settle(which, sems):
        settle(held[which].at[0, pl.ds(0, dp_count - 1)], sems.at[which])

    def shard_start(which):
        block = held[which].at[my_shard]
        for off in range(1, shard_count):
            place = (my_dp, shard_peer(off))
            remote(block, shard_send.at[which], shard_recv.at[which], place).start()

    def shard_settle(which, sems):
        settle(held[which].at[pl.ds(0, shard_count - 1)], sems.at[which])

    everyone = [
        (far, off)
        for far in range(dp_count)
        for off in range(shard_count)
        if (far, off) != (0, 0)
    ][::-1]
    mine = my_shard * dp_count + my_dp

    def all_start(text):
        block = long_queries.at[text, mine]
        for far, off in everyone:
            place = (dp_peer(far), shard_peer(off))
            remote(block, all_send.at[text], all_recv.at[text], place).start()

    def all_settle(text, sems):
        settle(long_queries.at[text, pl.ds(0, devices - 1)], sems.at[text])

    def unfold(block, rank, count):
        rows = pl.ds(rank * devices, count * devices)
        wide_queries[rows] = block.astype(jnp.float32).reshape(count * devices, pieces, LANES)
        for piece in range(pieces):
            slot_queries[rows, piece * LANES : (piece + 1) * LANES] = wide_queries[
                rows, piece, :
            ].astype(jnp.bfloat16)

    def picked(rank, count):
        rows = slice(rank * devices, (rank + count) * devices)
        return jnp.dot(
            pick_ref[:, rows], slot_queries[rows, :], preferred_element_type=jnp.float32
        )

    barrier = pltpu.get_barrier_semaphore()
    for far, off in everyone:
        pl.semaphore_signal(
            barrier,
            inc=1,
            device_id=(dp_peer(far), shard_peer(off)),
            device_id_type=pl.DeviceIdType.MESH,
        )
    queries[my_shard, my_dp] = short_queries[...].astype(jnp.bfloat16)
    cands[my_shard, my_dp] = meta_ref[...]

    states = long_states[...]
    rows = pl.ds(0, long_count * seq_len)
    pl.semaphore_wait(barrier, devices - 1)
    dp_start(0)
    dp_start(1)
    project(states, qkv_weight, qkv_bias_ref, qkv_ref, rows, 0)
    project(states, qkv_weight, qkv_bias_ref, qkv_ref, rows, 1)
    project(states, qkv_weight, qkv_bias_ref, qkv_ref, rows, 2)
    for which in (0, 1):
        dp_settle(which, dp_recv)
        shard_start(which)

    for text in range(long_count):
        start, rank = text * seq_len, short_count + text
        text_len = meta_ref[half:, LEN_LANE + rank : LEN_LANE + rank + 1]
        attend(qkv_ref, context_ref, start, seq_len, seq_len, text_len)
        here = pl.ds(start, seq_len)
        normed = normalise(long_states[here, :], context_ref[here, :], out_weight, out_bias_ref)
        row = lax.broadcasted_iota(jnp.int32, (seq_len, 1), 0)
        total = jnp.sum(jnp.where(row < text_len, normed, 0.0), axis=0, keepdims=True)
        query = embed(total, text_len.astype(jnp.float32), gain_ref, shift_ref)
        for piece in range(pieces):
            fold_ref[piece : piece + 1, :] = query[:, piece * LANES : (piece + 1) * LANES]
        long_queries[text, mine] = fold_ref[...].astype(jnp.bfloat16)
        all_start(text)

    shard_settle(0, shard_recv)
    shard_settle(1, shard_recv)
    grouped = cands[...].reshape(devices, PACK, LANES)
    entry = lax.broadcasted_iota(jnp.int32, (1, compact), 1)
    block = entry % devices
    texts = ((block % dp_count) * shard_count + block // dp_count) * text_dev + entry // devices
    ids = jnp.concatenate(
        [grouped[:, half, rank : rank + 1] for rank in range(text_dev)], axis=0
    )
    pick_ref[...] = jnp.where(ids == texts, 1.0, 0.0).T.astype(jnp.bfloat16)
    for rank in range(short_count):
        unfold(queries[:, :, rank], rank, 1)
    for text in range(long_count - 1):
        all_settle(text, all_recv)
        unfold(long_queries[text], short_count + text, 1)
    first_part = picked(0, text_dev - 1)
    all_settle(long_count - 1, all_recv)
    unfold(long_queries[long_count - 1], text_dev - 1, 1)
    text_queries[...] = (first_part + picked(text_dev - 1, 1)).astype(jnp.bfloat16)

    rows_here = index_rows.shape[0]
    cand_count = LANES // 2
    local = jnp.concatenate([grouped[:, line, :] for line in range(half)], axis=0) - me * rows_here
    local = jnp.concatenate([local, pltpu.roll(local, cand_count, 1)], axis=0)
    group = local >> 7
    lane = local & (LANES - 1)
    total = jnp.zeros((compact, LANES), jnp.float32)
    rows_step = 1024
    for step in range(rows_here // rows_step):
        scores = lax.dot_general(
            text_queries[...],
            index_rows[step * rows_step : (step + 1) * rows_step, :],
            (((1,), (1,)), ((), ())),
            preferred_element_type=jnp.float32,
        )
        for part in range(rows_step // LANES):
            found = jnp.take_along_axis(
                scores[:, part * LANES : (part + 1) * LANES],
                lane,
                axis=1,
                mode="promise_in_bounds",
            )
            total = jnp.where(group == step * (rows_step // LANES) + part, found, total)

    low = lax.broadcasted_iota(jnp.int32, (half * devices, LANES), 1) < cand_count
    packed = jnp.where(
        low, total[: half * devices], pltpu.roll(total[half * devices :], cand_count, 1)
    )
    for line in range(half):
        terms[:, line, :] = packed[line * devices : (line + 1) * devices]

    for far, off in everyone:
        pltpu.make_async_remote_copy(
            src_ref=terms.at[shard_peer(off) * dp_count + dp_peer(far)],
            dst_ref=arrived.at[far * shard_count + off],
            send_sem=out_send,
            recv_sem=out_recv,
            device_id=(dp_peer(far), shard_peer(off)),
            device_id_type=pl.DeviceIdType.MESH,
        ).start()
    for which in (0, 1):
        dp_settle(which, dp_send)
        shard_settle(which, shard_send)
    for text in range(long_count):
        all_settle(text, all_send)
    others = arrived.at[pl.ds(1, devices - 1)]
    settle(others, out_recv)
    result = terms[mine] + jnp.sum(others[...], axis=0)
    out_ref[:half, :] = result[:half, :cand_count]
    out_ref[half:, :] = result[:half, cand_count:]
    settle(others, out_send)


def shards(
    hidden,
    lengths,
    dealing,
    candidates,
    index_rows,
    qkv_weight,
    qkv_bias,
    out_weight,
    out_bias,
    norm_gain,
    norm_shift,
):
    text_dev, seq_len, width = hidden.shape
    dp_count, shard_count = lax.axis_size("dp"), lax.axis_size("shard")
    devices = dp_count * shard_count
    compact = devices * text_dev
    pieces = width // LANES
    hbm = pl.BlockSpec(memory_space=pl.ANY)
    vmem = pl.BlockSpec(memory_space=pltpu.VMEM)
    small = (qkv_bias[None, :], out_bias[None, :], norm_gain[None, :], norm_shift[None, :])
    long_count = text_dev // 3
    short_count = text_dev - long_count
    room, long_rows = short_count * seq_len, long_count * seq_len

    held = pl.pallas_call(
        functools.partial(encode_kernel, shard_count),
        in_specs=[hbm] * 11,
        out_specs=[vmem] * 10,
        out_shape=[
            pltpu.VMEM((short_count, pieces, LANES), jnp.float32),
            pltpu.VMEM((PACK, LANES), jnp.int32),
            pltpu.VMEM((1, 3 * width), jnp.float32),
            *[pltpu.VMEM((1, width), jnp.float32)] * 3,
            pltpu.VMEM((long_rows, width), jnp.bfloat16),
            pltpu.VMEM((width, 3 * width), jnp.bfloat16),
            pltpu.VMEM((width, width), jnp.bfloat16),
            pltpu.VMEM(index_rows.shape, jnp.bfloat16),
        ],
        scratch_shapes=[
            pltpu.VMEM((room, width), jnp.bfloat16),
            pltpu.VMEM((room, 3 * width), jnp.bfloat16),
            pltpu.VMEM((room, width), jnp.bfloat16),
            pltpu.VMEM((SLOTS, width), jnp.float32),
            pltpu.SMEM(lengths.shape, jnp.int32),
            pltpu.SMEM(dealing.shape, jnp.int32),
            pltpu.VMEM(candidates.shape, jnp.int32),
            pltpu.SemaphoreType.DMA((5,)),
            pltpu.SemaphoreType.DMA((text_dev,)),
            pltpu.SemaphoreType.DMA((7,)),
        ],
        compiler_params=pltpu.CompilerParams(vmem_limit_bytes=40 << 20),
        name="encode",
    )(lengths, dealing, candidates, *small, hidden, qkv_weight, out_weight, index_rows)

    return pl.pallas_call(
        functools.partial(finish_kernel, dp_count, shard_count),
        in_specs=[vmem] * 10,
        out_specs=vmem,
        out_shape=pltpu.VMEM(candidates.shape, jnp.float32),
        scratch_shapes=[
            pltpu.VMEM((long_rows, 3 * width), jnp.bfloat16),
            pltpu.VMEM((long_rows, width), jnp.bfloat16),
            pltpu.VMEM((pieces, LANES), jnp.float32),
            pltpu.VMEM((shard_count, dp_count, short_count, pieces, LANES), jnp.bfloat16),
            pltpu.VMEM((long_count, devices, pieces, LANES), jnp.bfloat16),
            pltpu.VMEM((shard_count, dp_count, PACK, LANES), jnp.int32),
            pltpu.VMEM((compact, pieces, LANES), jnp.float32),
            pltpu.VMEM((compact, width), jnp.bfloat16),
            pltpu.VMEM((compact, width), jnp.bfloat16),
            pltpu.VMEM((compact, compact), jnp.bfloat16),
            pltpu.VMEM((devices, PACK, LANES), jnp.float32),
            pltpu.VMEM((devices, PACK, LANES), jnp.float32),
            *[pltpu.SemaphoreType.DMA((2,))] * 4,
            *[pltpu.SemaphoreType.DMA((long_count,))] * 2,
            *[pltpu.SemaphoreType.DMA] * 2,
        ],
        compiler_params=pltpu.CompilerParams(
            vmem_limit_bytes=40 << 20, collective_id=0, has_side_effects=True
        ),
        name="finish",
    )(*[pltpu.with_memory_space_constraint(x, pltpu.VMEM) for x in held])


def solution(mesh):
    in_specs = (
        P(("dp", "shard"), None, None),
        P(),
        P(),
        P(("dp", "shard"), None),
        P(("dp", "shard"), None),
        P(),
        P(),
        P(),
        P(),
        P(),
        P(),
    )
    out_specs = P(("dp", "shard"), None)
    return jax.shard_map(shards, mesh=mesh, in_specs=in_specs, out_specs=out_specs, check_vma=False)
```

```python
import functools

import jax
import jax.numpy as jnp
from jax import lax
from jax.experimental import pallas as pl
from jax.experimental.pallas import tpu as pltpu
from jax.sharding import PartitionSpec as P

HEADS = 16
HEAD = 64
LANES = 128
SLOTS = 8
GRAIN = 16
UNIT = 128
PACK = 4
LEN_LANE = 64


def attend(qkv_ref, context_ref, start, rows, keys_count, text_len):
    width = context_ref.shape[1]
    queries, keys = pl.ds(start, rows), pl.ds(start, keys_count)
    lane = lax.broadcasted_iota(jnp.int32, (keys_count, LANES), 1)
    place = lax.broadcasted_iota(jnp.int32, (keys_count, LANES), 0)
    first = lane < HEAD
    valid = place < text_len
    key_valid = lax.broadcasted_iota(jnp.int32, (1, keys_count), 1) < text_len
    zero = jnp.zeros((keys_count, LANES), jnp.bfloat16)
    ones = jnp.ones((keys_count, LANES), jnp.bfloat16)
    ones_a, ones_b = jnp.where(first, ones, zero), jnp.where(first, zero, ones)
    first_valid, second_valid = first & valid, jnp.logical_not(first) & valid
    logits = []
    for base in range(0, width, LANES):
        q2 = qkv_ref[queries, base : base + LANES]
        k2 = qkv_ref[keys, width + base : width + base + LANES]
        for part in (jnp.where(first, k2, zero), jnp.where(first, zero, k2)):
            logits.append(
                lax.dot_general(
                    q2, part, (((1,), (1,)), ((), ())), preferred_element_type=jnp.float32
                )
            )
    probs = []
    for part in logits:
        part = jnp.where(key_valid, part, -1e30)
        peak = jnp.max(part, axis=-1, keepdims=True)
        probs.append(jnp.exp(part - peak).astype(jnp.bfloat16))
    for pair, base in enumerate(range(0, width, LANES)):
        v2 = qkv_ref[keys, 2 * width + base : 2 * width + base + LANES]
        both = jnp.concatenate(probs[2 * pair : 2 * pair + 2], axis=1)
        values = jnp.concatenate(
            [
                jnp.concatenate([jnp.where(first_valid, v2, zero), ones_a], axis=1),
                jnp.concatenate([jnp.where(second_valid, v2, zero), ones_b], axis=1),
            ],
            axis=0,
        )
        mixed = jnp.dot(both, values, preferred_element_type=jnp.float32)
        context_ref[queries, base : base + LANES] = (mixed[:, :LANES] / mixed[:, LANES:]).astype(
            jnp.bfloat16
        )


def project(states, qkv_weight, bias_ref, qkv_ref, rows, part, beside=None):
    width = states.shape[1]
    chunk = 512
    for start in range(part * width, (part + 1) * width, chunk):
        cols = slice(start, start + chunk)
        out = (
            jnp.dot(states, qkv_weight[:, cols], preferred_element_type=jnp.float32)
            + bias_ref[:, cols]
        )
        if part == 0:
            out = out * (1.0 / HEAD**0.5)
        qkv_ref[rows, cols] = out.astype(jnp.bfloat16)
        if beside is not None:
            beside(start, chunk)


def normalise(states, context, out_weight, out_bias_ref):
    resid = (
        states.astype(jnp.float32)
        + jnp.dot(context, out_weight[...], preferred_element_type=jnp.float32)
        + out_bias_ref[...]
    )
    centre = jnp.mean(resid, axis=-1, keepdims=True)
    resid = resid - centre
    spread = jnp.mean(resid * resid, axis=-1, keepdims=True)
    return resid * lax.rsqrt(spread + 1e-05)


def embed(total, count, gain_ref, shift_ref):
    pooled = total / count * gain_ref[...] + shift_ref[...]
    return pooled * lax.rsqrt(jnp.sum(pooled * pooled, axis=-1, keepdims=True) + 1e-06)


def encode_kernel(
    shard_count,
    lengths_hbm,
    dealing_hbm,
    cand_hbm,
    qkv_bias_hbm,
    out_bias_hbm,
    gain_hbm,
    shift_hbm,
    hidden_hbm,
    qkv_weight_hbm,
    out_weight_hbm,
    index_hbm,
    queries_ref,
    meta_ref,
    qkv_bias_ref,
    out_bias_ref,
    gain_ref,
    shift_ref,
    long_states,
    qkv_weight,
    out_weight,
    index_rows,
    states_ref,
    qkv_ref,
    context_ref,
    fold_ref,
    lengths_ref,
    dealing_ref,
    cand_ref,
    load_sems,
    state_sems,
    small_sems,
):
    text_dev, seq_len, width = hidden_hbm.shape
    loads = [
        pltpu.make_async_copy(
            qkv_weight_hbm.at[:, pl.ds(part * width, width)],
            qkv_weight.at[:, pl.ds(part * width, width)],
            load_sems.at[part],
        )
        for part in range(3)
    ]
    smalls = [
        pltpu.make_async_copy(source, target, small_sems.at[place])
        for place, (source, target) in enumerate(
            [
                (lengths_hbm, lengths_ref),
                (dealing_hbm, dealing_ref),
                (cand_hbm, cand_ref),
                (qkv_bias_hbm, qkv_bias_ref),
                (out_bias_hbm, out_bias_ref),
                (gain_hbm, gain_ref),
                (shift_hbm, shift_ref),
            ]
        )
    ]
    for small in smalls:
        small.start()
    for load in loads:
        load.start()
    for small in smalls[:2]:
        small.wait()
    me = lax.axis_index("dp") * shard_count + lax.axis_index("shard")
    texts = [dealing_ref[me * text_dev + slot] for slot in range(text_dev)]
    counts = [lengths_ref[text] for text in texts]
    ranks = []
    for slot in range(text_dev):
        rank = jnp.int32(0)
        for other in range(text_dev):
            if other < slot:
                rank = rank + jnp.where(counts[other] <= counts[slot], 1, 0)
            if other > slot:
                rank = rank + jnp.where(counts[other] < counts[slot], 1, 0)
        ranks.append(rank)

    def by_rank(values):
        out = []
        for rank in range(text_dev):
            value = values[0]
            for slot in range(1, text_dev):
                value = jnp.where(ranks[slot] == rank, values[slot], value)
            out.append(value)
        return out

    slots = by_rank(list(range(text_dev)))
    texts = by_rank(texts)
    counts = by_rank(counts)
    short_count = text_dev - long_states.shape[0] // seq_len
    starts, sizes = [], []
    total_rows = jnp.int32(0)
    for rank in range(short_count):
        size = (counts[rank] + GRAIN - 1) // GRAIN * GRAIN
        starts.append(total_rows)
        sizes.append(size)
        total_rows = total_rows + size

    def state_copy(rank):
        size = pl.multiple_of(sizes[rank], GRAIN)
        return pltpu.make_async_copy(
            hidden_hbm.at[slots[rank], pl.ds(0, size)],
            states_ref.at[pl.ds(pl.multiple_of(starts[rank], GRAIN), size)],
            state_sems.at[rank],
        )

    def long_copy(rank):
        return pltpu.make_async_copy(
            hidden_hbm.at[slots[rank]],
            long_states.at[pl.ds((rank - short_count) * seq_len, seq_len)],
            state_sems.at[rank],
        )

    loads.append(pltpu.make_async_copy(out_weight_hbm, out_weight, load_sems.at[3]))
    loads += [long_copy(rank) for rank in range(short_count, text_dev)]
    loads.append(pltpu.make_async_copy(index_hbm, index_rows, load_sems.at[4]))

    for rank in range(short_count):
        state_copy(rank).start()
    for small in smalls[2:]:
        small.wait()
    half = text_dev // 2
    meta_ref[:half, :] = jnp.concatenate([cand_ref[:half, :], cand_ref[half:, :]], axis=1)
    lane = lax.broadcasted_iota(jnp.int32, (1, LANES), 1)
    row = jnp.zeros_like(lane)
    for rank in range(text_dev):
        row = jnp.where(lane == rank, texts[rank], row)
        row = jnp.where(lane == LEN_LANE + rank, counts[rank], row)
    meta_ref[half:, :] = row
    for rank in range(short_count):
        state_copy(rank).wait()

    units = (total_rows + UNIT - 1) // UNIT
    full, rest = units // PACK, lax.rem(units, PACK)

    def over_rows(body):
        def step(i, carry):
            body(pl.multiple_of(i * (PACK * UNIT), PACK * UNIT), PACK * UNIT)
            return carry

        lax.fori_loop(0, full, step, 0)
        for size in range(1, PACK):
            pl.when(rest == size)(
                lambda size=size: body(
                    pl.multiple_of(full * (PACK * UNIT), PACK * UNIT), size * UNIT
                )
            )

    for part in range(3):
        loads[part].wait()
        if part == 2:
            for load in loads[3:]:
                load.start()

        def qkv_block(base, size):
            rows = pl.ds(base, size)
            project(states_ref[rows, :], qkv_weight, qkv_bias_ref, qkv_ref, rows, part)

        over_rows(qkv_block)

    def text_step(rank, carry):
        count, start = counts[0], starts[0]
        for other in range(1, short_count):
            count = jnp.where(rank == other, counts[other], count)
            start = jnp.where(rank == other, starts[other], start)
        start = pl.multiple_of(start, GRAIN)
        small = count <= 128
        large = count > 192

        @pl.when(small)
        def _():
            attend(qkv_ref, context_ref, start, 128, 128, count)

        @pl.when(jnp.logical_not(small | large))
        def _():
            attend(qkv_ref, context_ref, start, 192, 256, count)

        @pl.when(large)
        def _():
            attend(qkv_ref, context_ref, start, 256, 256, count)

        return carry

    lax.fori_loop(0, short_count, text_step, 0)

    loads[3].wait()
    slot_id = lax.broadcasted_iota(jnp.int32, (SLOTS, 1), 0)
    start_col = jnp.zeros((SLOTS, 1), jnp.int32)
    count_col = jnp.zeros((SLOTS, 1), jnp.int32)
    for rank in range(short_count):
        here = slot_id == rank
        start_col = jnp.where(here, starts[rank], start_col)
        count_col = jnp.where(here, counts[rank], count_col)
    fold_ref[...] = jnp.zeros_like(fold_ref)

    def out_block(base, size):
        rows = pl.ds(base, size)
        normed = normalise(states_ref[rows, :], context_ref[rows, :], out_weight, out_bias_ref)
        row = lax.broadcasted_iota(jnp.int32, (size, 1), 0) + base
        normed = jnp.where(row < total_rows, normed, 0.0).astype(jnp.bfloat16)
        place = lax.broadcasted_iota(jnp.int32, (SLOTS, size), 1) + base - start_col
        member = (place >= 0) & (place < count_col)
        fold_ref[...] += jnp.dot(
            jnp.where(member, 1.0, 0.0).astype(jnp.bfloat16),
            normed,
            preferred_element_type=jnp.float32,
        )

    over_rows(out_block)
    query = embed(
        fold_ref[...], jnp.maximum(count_col, 1).astype(jnp.float32), gain_ref, shift_ref
    )
    pieces = width // LANES
    for slot in range(short_count):
        for piece in range(pieces):
            queries_ref[slot, piece : piece + 1, :] = query[
                slot : slot + 1, piece * LANES : (piece + 1) * LANES
            ]
    for load in loads[4:]:
        load.wait()


def finish_kernel(
    dp_count,
    shard_count,
    short_queries,
    meta_ref,
    qkv_bias_ref,
    out_bias_ref,
    gain_ref,
    shift_ref,
    long_states,
    qkv_weight,
    out_weight,
    index_rows,
    out_ref,
    index_turned,
    qkv_ref,
    context_ref,
    fold_ref,
    queries,
    long_queries,
    cands,
    wide_queries,
    slot_queries,
    text_queries,
    pick_ref,
    terms,
    arrived,
    dp_send,
    dp_recv,
    shard_send,
    shard_recv,
    all_send,
    all_recv,
    out_send,
    out_recv,
):
    my_dp, my_shard = lax.axis_index("dp"), lax.axis_index("shard")
    me = my_dp * shard_count + my_shard
    width = long_states.shape[1]
    short_count, pieces = short_queries.shape[:2]
    text_dev = out_ref.shape[0]
    long_count = text_dev - short_count
    seq_len = long_states.shape[0] // long_count
    devices = dp_count * shard_count
    compact = devices * text_dev
    half = text_dev // 2

    def dp_peer(off):
        return lax.rem(my_dp + off, dp_count)

    def shard_peer(off):
        return lax.rem(my_shard + off, shard_count)

    def remote(block, send, recv, device):
        return pltpu.make_async_remote_copy(
            src_ref=block,
            dst_ref=block,
            send_sem=send,
            recv_sem=recv,
            device_id=device,
            device_id_type=pl.DeviceIdType.MESH,
        )

    held = [queries, cands]

    def settle(blocks, sem):
        pltpu.make_async_copy(blocks, blocks, sem).wait()

    def dp_start(which):
        block = held[which].at[my_shard, my_dp]
        for off in range(1, dp_count):
            place = (dp_peer(off), my_shard)
            remote(block, dp_send.at[which], dp_recv.at[which], place).start()

    def dp_settle(which, sems):
        settle(held[which].at[0, pl.ds(0, dp_count - 1)], sems.at[which])

    def shard_start(which):
        block = held[which].at[my_shard]
        for off in range(1, shard_count):
            place = (my_dp, shard_peer(off))
            remote(block, shard_send.at[which], shard_recv.at[which], place).start()

    def shard_settle(which, sems):
        settle(held[which].at[pl.ds(0, shard_count - 1)], sems.at[which])

    everyone = [
        (far, off)
        for far in range(dp_count)
        for off in range(shard_count)
        if (far, off) != (0, 0)
    ][::-1]
    mine = my_shard * dp_count + my_dp

    def all_start(text):
        block = long_queries.at[text, mine]
        for far, off in everyone:
            place = (dp_peer(far), shard_peer(off))
            remote(block, all_send.at[text], all_recv.at[text], place).start()

    def all_settle(text, sems):
        settle(long_queries.at[text, pl.ds(0, devices - 1)], sems.at[text])

    def unfold(block, rank, count):
        rows = pl.ds(rank * devices, count * devices)
        wide_queries[rows] = block.astype(jnp.float32).reshape(count * devices, pieces, LANES)
        for piece in range(pieces):
            slot_queries[rows, piece * LANES : (piece + 1) * LANES] = wide_queries[
                rows, piece, :
            ].astype(jnp.bfloat16)

    def picked(rank, count):
        rows = slice(rank * devices, (rank + count) * devices)
        return jnp.dot(
            pick_ref[:, rows], slot_queries[rows, :], preferred_element_type=jnp.float32
        )

    barrier = pltpu.get_barrier_semaphore()
    for far, off in everyone:
        pl.semaphore_signal(
            barrier,
            inc=1,
            device_id=(dp_peer(far), shard_peer(off)),
            device_id_type=pl.DeviceIdType.MESH,
        )
    queries[my_shard, my_dp] = short_queries[...].astype(jnp.bfloat16)
    cands[my_shard, my_dp] = meta_ref[...]

    states = long_states[...]
    rows = pl.ds(0, long_count * seq_len)
    tiles = index_rows.shape[0] // LANES

    def turn(start, chunk):
        first = start * tiles // (3 * width)
        last = (start + chunk) * tiles // (3 * width)
        for tile in range(first, last):
            block = slice(tile * LANES, (tile + 1) * LANES)
            index_turned[:, block] = index_rows[block, :].T

    for part in range(3):
        project(states, qkv_weight, qkv_bias_ref, qkv_ref, rows, part, turn)
    pl.semaphore_wait(barrier, devices - 1)
    dp_start(0)
    dp_start(1)

    for text in range(long_count):
        start, rank = text * seq_len, short_count + text
        text_len = meta_ref[half:, LEN_LANE + rank : LEN_LANE + rank + 1]
        attend(qkv_ref, context_ref, start, seq_len, seq_len, text_len)
        here = pl.ds(start, seq_len)
        normed = normalise(long_states[here, :], context_ref[here, :], out_weight, out_bias_ref)
        row = lax.broadcasted_iota(jnp.int32, (seq_len, 1), 0)
        total = jnp.sum(jnp.where(row < text_len, normed, 0.0), axis=0, keepdims=True)
        query = embed(total, text_len.astype(jnp.float32), gain_ref, shift_ref)
        for piece in range(pieces):
            fold_ref[piece : piece + 1, :] = query[:, piece * LANES : (piece + 1) * LANES]
        long_queries[text, mine] = fold_ref[...].astype(jnp.bfloat16)
        all_start(text)
        if text == 0:
            for which in (0, 1):
                dp_settle(which, dp_recv)
                shard_start(which)

    shard_settle(0, shard_recv)
    shard_settle(1, shard_recv)
    grouped = cands[...].reshape(devices, PACK, LANES)
    entry = lax.broadcasted_iota(jnp.int32, (1, compact), 1)
    block = entry % devices
    texts = ((block % dp_count) * shard_count + block // dp_count) * text_dev + entry // devices
    ids = jnp.concatenate(
        [grouped[:, half, rank : rank + 1] for rank in range(text_dev)], axis=0
    )
    pick_ref[...] = jnp.where(ids == texts, 1.0, 0.0).T.astype(jnp.bfloat16)
    for rank in range(short_count):
        unfold(queries[:, :, rank], rank, 1)
    for text in range(long_count - 1):
        all_settle(text, all_recv)
        unfold(long_queries[text], short_count + text, 1)
    first_part = picked(0, text_dev - 1)
    all_settle(long_count - 1, all_recv)
    unfold(long_queries[long_count - 1], text_dev - 1, 1)
    text_queries[...] = (first_part + picked(text_dev - 1, 1)).astype(jnp.bfloat16)

    rows_here = index_rows.shape[0]
    cand_count = LANES // 2
    local = jnp.concatenate([grouped[:, line, :] for line in range(half)], axis=0) - me * rows_here
    local = jnp.concatenate([local, pltpu.roll(local, cand_count, 1)], axis=0)
    group = local >> 7
    lane = local & (LANES - 1)
    total = jnp.zeros((compact, LANES), jnp.float32)
    rows_step = 1024
    for step in range(rows_here // rows_step):
        scores = jnp.dot(
            text_queries[...],
            index_turned[:, step * rows_step : (step + 1) * rows_step],
            preferred_element_type=jnp.float32,
        )
        for part in range(rows_step // LANES):
            found = jnp.take_along_axis(
                scores[:, part * LANES : (part + 1) * LANES],
                lane,
                axis=1,
                mode="promise_in_bounds",
            )
            total = jnp.where(group == step * (rows_step // LANES) + part, found, total)

    low = lax.broadcasted_iota(jnp.int32, (half * devices, LANES), 1) < cand_count
    packed = jnp.where(
        low, total[: half * devices], pltpu.roll(total[half * devices :], cand_count, 1)
    )
    for line in range(half):
        terms[:, line, :] = packed[line * devices : (line + 1) * devices]

    for far, off in everyone:
        pltpu.make_async_remote_copy(
            src_ref=terms.at[shard_peer(off) * dp_count + dp_peer(far)],
            dst_ref=arrived.at[far * shard_count + off],
            send_sem=out_send,
            recv_sem=out_recv,
            device_id=(dp_peer(far), shard_peer(off)),
            device_id_type=pl.DeviceIdType.MESH,
        ).start()
    for which in (0, 1):
        dp_settle(which, dp_send)
        shard_settle(which, shard_send)
    for text in range(long_count):
        all_settle(text, all_send)
    others = arrived.at[pl.ds(1, devices - 1)]
    settle(others, out_recv)
    result = terms[mine] + jnp.sum(others[...], axis=0)
    out_ref[:half, :] = result[:half, :cand_count]
    out_ref[half:, :] = result[:half, cand_count:]
    settle(others, out_send)


def shards(
    hidden,
    lengths,
    dealing,
    candidates,
    index_rows,
    qkv_weight,
    qkv_bias,
    out_weight,
    out_bias,
    norm_gain,
    norm_shift,
):
    text_dev, seq_len, width = hidden.shape
    dp_count, shard_count = lax.axis_size("dp"), lax.axis_size("shard")
    devices = dp_count * shard_count
    compact = devices * text_dev
    pieces = width // LANES
    hbm = pl.BlockSpec(memory_space=pl.ANY)
    vmem = pl.BlockSpec(memory_space=pltpu.VMEM)
    small = (qkv_bias[None, :], out_bias[None, :], norm_gain[None, :], norm_shift[None, :])
    long_count = text_dev // 3
    short_count = text_dev - long_count
    room, long_rows = short_count * seq_len, long_count * seq_len

    held = pl.pallas_call(
        functools.partial(encode_kernel, shard_count),
        in_specs=[hbm] * 11,
        out_specs=[vmem] * 10,
        out_shape=[
            pltpu.VMEM((short_count, pieces, LANES), jnp.float32),
            pltpu.VMEM((PACK, LANES), jnp.int32),
            pltpu.VMEM((1, 3 * width), jnp.float32),
            *[pltpu.VMEM((1, width), jnp.float32)] * 3,
            pltpu.VMEM((long_rows, width), jnp.bfloat16),
            pltpu.VMEM((width, 3 * width), jnp.bfloat16),
            pltpu.VMEM((width, width), jnp.bfloat16),
            pltpu.VMEM(index_rows.shape, jnp.bfloat16),
        ],
        scratch_shapes=[
            pltpu.VMEM((room, width), jnp.bfloat16),
            pltpu.VMEM((room, 3 * width), jnp.bfloat16),
            pltpu.VMEM((room, width), jnp.bfloat16),
            pltpu.VMEM((SLOTS, width), jnp.float32),
            pltpu.SMEM(lengths.shape, jnp.int32),
            pltpu.SMEM(dealing.shape, jnp.int32),
            pltpu.VMEM(candidates.shape, jnp.int32),
            pltpu.SemaphoreType.DMA((5,)),
            pltpu.SemaphoreType.DMA((text_dev,)),
            pltpu.SemaphoreType.DMA((7,)),
        ],
        compiler_params=pltpu.CompilerParams(vmem_limit_bytes=40 << 20),
        name="encode",
    )(lengths, dealing, candidates, *small, hidden, qkv_weight, out_weight, index_rows)

    return pl.pallas_call(
        functools.partial(finish_kernel, dp_count, shard_count),
        in_specs=[vmem] * 10,
        out_specs=vmem,
        out_shape=pltpu.VMEM(candidates.shape, jnp.float32),
        scratch_shapes=[
            pltpu.VMEM((width, index_rows.shape[0]), jnp.bfloat16),
            pltpu.VMEM((long_rows, 3 * width), jnp.bfloat16),
            pltpu.VMEM((long_rows, width), jnp.bfloat16),
            pltpu.VMEM((pieces, LANES), jnp.float32),
            pltpu.VMEM((shard_count, dp_count, short_count, pieces, LANES), jnp.bfloat16),
            pltpu.VMEM((long_count, devices, pieces, LANES), jnp.bfloat16),
            pltpu.VMEM((shard_count, dp_count, PACK, LANES), jnp.int32),
            pltpu.VMEM((compact, pieces, LANES), jnp.float32),
            pltpu.VMEM((compact, width), jnp.bfloat16),
            pltpu.VMEM((compact, width), jnp.bfloat16),
            pltpu.VMEM((compact, compact), jnp.bfloat16),
            pltpu.VMEM((devices, PACK, LANES), jnp.float32),
            pltpu.VMEM((devices, PACK, LANES), jnp.float32),
            *[pltpu.SemaphoreType.DMA((2,))] * 4,
            *[pltpu.SemaphoreType.DMA((long_count,))] * 2,
            *[pltpu.SemaphoreType.DMA] * 2,
        ],
        compiler_params=pltpu.CompilerParams(
            vmem_limit_bytes=40 << 20, collective_id=0, has_side_effects=True
        ),
        name="finish",
    )(*[pltpu.with_memory_space_constraint(x, pltpu.VMEM) for x in held])


def solution(mesh):
    in_specs = (
        P(("dp", "shard"), None, None),
        P(),
        P(),
        P(("dp", "shard"), None),
        P(("dp", "shard"), None),
        P(),
        P(),
        P(),
        P(),
        P(),
        P(),
    )
    out_specs = P(("dp", "shard"), None)
    return jax.shard_map(shards, mesh=mesh, in_specs=in_specs, out_specs=out_specs, check_vma=False)
```

```python
import functools

import jax
import jax.numpy as jnp
from jax import lax
from jax.experimental import pallas as pl
from jax.experimental.pallas import tpu as pltpu
from jax.sharding import PartitionSpec as P

HEADS = 16
HEAD = 64
LANES = 128
SLOTS = 8
GRAIN = 16
UNIT = 128
PACK = 4
QKV_PASS = 6
OUT_PASS = 4
LEN_LANE = 64


def attend(qkv_ref, context_ref, start, rows, keys_count, text_len):
    width = context_ref.shape[1]
    queries, keys = pl.ds(start, rows), pl.ds(start, keys_count)
    lane = lax.broadcasted_iota(jnp.int32, (keys_count, LANES), 1)
    place = lax.broadcasted_iota(jnp.int32, (keys_count, LANES), 0)
    first = lane < HEAD
    valid = place < text_len
    key_valid = lax.broadcasted_iota(jnp.int32, (1, keys_count), 1) < text_len
    zero = jnp.zeros((keys_count, LANES), jnp.bfloat16)
    ones = jnp.ones((keys_count, LANES), jnp.bfloat16)
    ones_a, ones_b = jnp.where(first, ones, zero), jnp.where(first, zero, ones)
    first_valid, second_valid = first & valid, jnp.logical_not(first) & valid
    logits = []
    for base in range(0, width, LANES):
        q2 = qkv_ref[queries, base : base + LANES]
        k2 = qkv_ref[keys, width + base : width + base + LANES]
        for part in (jnp.where(first, k2, zero), jnp.where(first, zero, k2)):
            logits.append(
                lax.dot_general(
                    q2, part, (((1,), (1,)), ((), ())), preferred_element_type=jnp.float32
                )
            )
    probs = []
    for part in logits:
        part = jnp.where(key_valid, part, -1e30)
        peak = jnp.max(part, axis=-1, keepdims=True)
        probs.append(jnp.exp(part - peak).astype(jnp.bfloat16))
    for pair, base in enumerate(range(0, width, LANES)):
        v2 = qkv_ref[keys, 2 * width + base : 2 * width + base + LANES]
        both = jnp.concatenate(probs[2 * pair : 2 * pair + 2], axis=1)
        values = jnp.concatenate(
            [
                jnp.concatenate([jnp.where(first_valid, v2, zero), ones_a], axis=1),
                jnp.concatenate([jnp.where(second_valid, v2, zero), ones_b], axis=1),
            ],
            axis=0,
        )
        mixed = jnp.dot(both, values, preferred_element_type=jnp.float32)
        context_ref[queries, base : base + LANES] = (mixed[:, :LANES] / mixed[:, LANES:]).astype(
            jnp.bfloat16
        )


def project(states, qkv_weight, bias_ref, qkv_ref, rows, part, beside=None):
    width = states.shape[1]
    chunk = 512
    for start in range(part * width, (part + 1) * width, chunk):
        cols = slice(start, start + chunk)
        out = (
            jnp.dot(states, qkv_weight[:, cols], preferred_element_type=jnp.float32)
            + bias_ref[:, cols]
        )
        if part == 0:
            out = out * (1.0 / HEAD**0.5)
        qkv_ref[rows, cols] = out.astype(jnp.bfloat16)
        if beside is not None:
            beside(start, chunk)


def normalise(states, context, out_weight, out_bias_ref):
    resid = (
        states.astype(jnp.float32)
        + jnp.dot(context, out_weight[...], preferred_element_type=jnp.float32)
        + out_bias_ref[...]
    )
    centre = jnp.mean(resid, axis=-1, keepdims=True)
    resid = resid - centre
    spread = jnp.mean(resid * resid, axis=-1, keepdims=True)
    return resid * lax.rsqrt(spread + 1e-05)


def embed(total, count, gain_ref, shift_ref):
    pooled = total / count * gain_ref[...] + shift_ref[...]
    return pooled * lax.rsqrt(jnp.sum(pooled * pooled, axis=-1, keepdims=True) + 1e-06)


def encode_kernel(
    shard_count,
    lengths_hbm,
    dealing_hbm,
    cand_hbm,
    qkv_bias_hbm,
    out_bias_hbm,
    gain_hbm,
    shift_hbm,
    hidden_hbm,
    qkv_weight_hbm,
    out_weight_hbm,
    index_hbm,
    queries_ref,
    meta_ref,
    qkv_bias_ref,
    out_bias_ref,
    gain_ref,
    shift_ref,
    long_states,
    qkv_weight,
    out_weight,
    index_rows,
    states_ref,
    qkv_ref,
    context_ref,
    fold_ref,
    lengths_ref,
    dealing_ref,
    cand_ref,
    load_sems,
    state_sems,
    small_sems,
):
    text_dev, seq_len, width = hidden_hbm.shape
    loads = [
        pltpu.make_async_copy(
            qkv_weight_hbm.at[:, pl.ds(part * width, width)],
            qkv_weight.at[:, pl.ds(part * width, width)],
            load_sems.at[part],
        )
        for part in range(3)
    ]
    smalls = [
        pltpu.make_async_copy(source, target, small_sems.at[place])
        for place, (source, target) in enumerate(
            [
                (lengths_hbm, lengths_ref),
                (dealing_hbm, dealing_ref),
                (cand_hbm, cand_ref),
                (qkv_bias_hbm, qkv_bias_ref),
                (out_bias_hbm, out_bias_ref),
                (gain_hbm, gain_ref),
                (shift_hbm, shift_ref),
            ]
        )
    ]
    for small in smalls:
        small.start()
    for load in loads:
        load.start()
    for small in smalls[:2]:
        small.wait()
    me = lax.axis_index("dp") * shard_count + lax.axis_index("shard")
    texts = [dealing_ref[me * text_dev + slot] for slot in range(text_dev)]
    counts = [lengths_ref[text] for text in texts]
    ranks = []
    for slot in range(text_dev):
        rank = jnp.int32(0)
        for other in range(text_dev):
            if other < slot:
                rank = rank + jnp.where(counts[other] <= counts[slot], 1, 0)
            if other > slot:
                rank = rank + jnp.where(counts[other] < counts[slot], 1, 0)
        ranks.append(rank)

    def by_rank(values):
        out = []
        for rank in range(text_dev):
            value = values[0]
            for slot in range(1, text_dev):
                value = jnp.where(ranks[slot] == rank, values[slot], value)
            out.append(value)
        return out

    slots = by_rank(list(range(text_dev)))
    texts = by_rank(texts)
    counts = by_rank(counts)
    short_count = text_dev - long_states.shape[0] // seq_len
    starts, sizes = [], []
    total_rows = jnp.int32(0)
    for rank in range(short_count):
        size = (counts[rank] + GRAIN - 1) // GRAIN * GRAIN
        starts.append(total_rows)
        sizes.append(size)
        total_rows = total_rows + size

    def state_copy(rank):
        size = pl.multiple_of(sizes[rank], GRAIN)
        return pltpu.make_async_copy(
            hidden_hbm.at[slots[rank], pl.ds(0, size)],
            states_ref.at[pl.ds(pl.multiple_of(starts[rank], GRAIN), size)],
            state_sems.at[rank],
        )

    def long_copy(rank):
        return pltpu.make_async_copy(
            hidden_hbm.at[slots[rank]],
            long_states.at[pl.ds((rank - short_count) * seq_len, seq_len)],
            state_sems.at[rank],
        )

    loads.append(pltpu.make_async_copy(out_weight_hbm, out_weight, load_sems.at[3]))
    loads += [long_copy(rank) for rank in range(short_count, text_dev)]
    loads.append(pltpu.make_async_copy(index_hbm, index_rows, load_sems.at[4]))

    for rank in range(short_count):
        state_copy(rank).start()
    for small in smalls[2:]:
        small.wait()
    half = text_dev // 2
    meta_ref[:half, :] = jnp.concatenate([cand_ref[:half, :], cand_ref[half:, :]], axis=1)
    lane = lax.broadcasted_iota(jnp.int32, (1, LANES), 1)
    row = jnp.zeros_like(lane)
    for rank in range(text_dev):
        row = jnp.where(lane == rank, texts[rank], row)
        row = jnp.where(lane == LEN_LANE + rank, counts[rank], row)
    meta_ref[half:, :] = row
    for rank in range(short_count):
        state_copy(rank).wait()

    units = (total_rows + UNIT - 1) // UNIT

    def over_rows(body, most):
        full, rest = units // most, lax.rem(units, most)

        def step(i, carry):
            body(pl.multiple_of(i * (most * UNIT), most * UNIT), most * UNIT)
            return carry

        lax.fori_loop(0, full, step, 0)
        for size in range(1, most):
            pl.when(rest == size)(
                lambda size=size: body(
                    pl.multiple_of(full * (most * UNIT), most * UNIT), size * UNIT
                )
            )

    for part in range(3):
        loads[part].wait()
        if part == 2:
            for load in loads[3:]:
                load.start()

        def qkv_block(base, size):
            rows = pl.ds(base, size)
            project(states_ref[rows, :], qkv_weight, qkv_bias_ref, qkv_ref, rows, part)

        over_rows(qkv_block, QKV_PASS)

    def text_step(rank, carry):
        count, start = counts[0], starts[0]
        for other in range(1, short_count):
            count = jnp.where(rank == other, counts[other], count)
            start = jnp.where(rank == other, starts[other], start)
        start = pl.multiple_of(start, GRAIN)
        small = count <= 128
        large = count > 192

        @pl.when(small)
        def _():
            attend(qkv_ref, context_ref, start, 128, 128, count)

        @pl.when(jnp.logical_not(small | large))
        def _():
            attend(qkv_ref, context_ref, start, 192, 256, count)

        @pl.when(large)
        def _():
            attend(qkv_ref, context_ref, start, 256, 256, count)

        return carry

    lax.fori_loop(0, short_count, text_step, 0)

    loads[3].wait()
    slot_id = lax.broadcasted_iota(jnp.int32, (SLOTS, 1), 0)
    start_col = jnp.zeros((SLOTS, 1), jnp.int32)
    count_col = jnp.zeros((SLOTS, 1), jnp.int32)
    for rank in range(short_count):
        here = slot_id == rank
        start_col = jnp.where(here, starts[rank], start_col)
        count_col = jnp.where(here, counts[rank], count_col)
    fold_ref[...] = jnp.zeros_like(fold_ref)

    def out_block(base, size):
        rows = pl.ds(base, size)
        normed = normalise(states_ref[rows, :], context_ref[rows, :], out_weight, out_bias_ref)
        row = lax.broadcasted_iota(jnp.int32, (size, 1), 0) + base
        normed = jnp.where(row < total_rows, normed, 0.0).astype(jnp.bfloat16)
        place = lax.broadcasted_iota(jnp.int32, (SLOTS, size), 1) + base - start_col
        member = (place >= 0) & (place < count_col)
        fold_ref[...] += jnp.dot(
            jnp.where(member, 1.0, 0.0).astype(jnp.bfloat16),
            normed,
            preferred_element_type=jnp.float32,
        )

    over_rows(out_block, OUT_PASS)
    query = embed(
        fold_ref[...], jnp.maximum(count_col, 1).astype(jnp.float32), gain_ref, shift_ref
    )
    pieces = width // LANES
    for slot in range(short_count):
        for piece in range(pieces):
            queries_ref[slot, piece : piece + 1, :] = query[
                slot : slot + 1, piece * LANES : (piece + 1) * LANES
            ]
    for load in loads[4:]:
        load.wait()


def finish_kernel(
    dp_count,
    shard_count,
    short_queries,
    meta_ref,
    qkv_bias_ref,
    out_bias_ref,
    gain_ref,
    shift_ref,
    long_states,
    qkv_weight,
    out_weight,
    index_rows,
    out_ref,
    index_turned,
    qkv_ref,
    context_ref,
    fold_ref,
    queries,
    long_queries,
    cands,
    wide_queries,
    slot_queries,
    text_queries,
    pick_ref,
    terms,
    arrived,
    dp_send,
    dp_recv,
    shard_send,
    shard_recv,
    all_send,
    all_recv,
    out_send,
    out_recv,
):
    my_dp, my_shard = lax.axis_index("dp"), lax.axis_index("shard")
    me = my_dp * shard_count + my_shard
    width = long_states.shape[1]
    short_count, pieces = short_queries.shape[:2]
    text_dev = out_ref.shape[0]
    long_count = text_dev - short_count
    seq_len = long_states.shape[0] // long_count
    devices = dp_count * shard_count
    compact = devices * text_dev
    half = text_dev // 2

    def dp_peer(off):
        return lax.rem(my_dp + off, dp_count)

    def shard_peer(off):
        return lax.rem(my_shard + off, shard_count)

    def remote(block, send, recv, device):
        return pltpu.make_async_remote_copy(
            src_ref=block,
            dst_ref=block,
            send_sem=send,
            recv_sem=recv,
            device_id=device,
            device_id_type=pl.DeviceIdType.MESH,
        )

    held = [queries, cands]

    def settle(blocks, sem):
        pltpu.make_async_copy(blocks, blocks, sem).wait()

    def dp_start(which):
        block = held[which].at[my_shard, my_dp]
        for off in range(1, dp_count):
            place = (dp_peer(off), my_shard)
            remote(block, dp_send.at[which], dp_recv.at[which], place).start()

    def dp_settle(which, sems):
        settle(held[which].at[0, pl.ds(0, dp_count - 1)], sems.at[which])

    def shard_start(which):
        block = held[which].at[my_shard]
        for off in range(1, shard_count):
            place = (my_dp, shard_peer(off))
            remote(block, shard_send.at[which], shard_recv.at[which], place).start()

    def shard_settle(which, sems):
        settle(held[which].at[pl.ds(0, shard_count - 1)], sems.at[which])

    everyone = [
        (far, off)
        for far in range(dp_count)
        for off in range(shard_count)
        if (far, off) != (0, 0)
    ][::-1]
    mine = my_shard * dp_count + my_dp

    def all_start(text):
        block = long_queries.at[text, mine]
        for far, off in everyone:
            place = (dp_peer(far), shard_peer(off))
            remote(block, all_send.at[text], all_recv.at[text], place).start()

    def all_settle(text, sems):
        settle(long_queries.at[text, pl.ds(0, devices - 1)], sems.at[text])

    def unfold(block, rank, count):
        rows = pl.ds(rank * devices, count * devices)
        wide_queries[rows] = block.astype(jnp.float32).reshape(count * devices, pieces, LANES)
        for piece in range(pieces):
            slot_queries[rows, piece * LANES : (piece + 1) * LANES] = wide_queries[
                rows, piece, :
            ].astype(jnp.bfloat16)

    def picked(rank, count):
        rows = slice(rank * devices, (rank + count) * devices)
        return jnp.dot(
            pick_ref[:, rows], slot_queries[rows, :], preferred_element_type=jnp.float32
        )

    barrier = pltpu.get_barrier_semaphore()
    for far, off in everyone:
        pl.semaphore_signal(
            barrier,
            inc=1,
            device_id=(dp_peer(far), shard_peer(off)),
            device_id_type=pl.DeviceIdType.MESH,
        )
    queries[my_shard, my_dp] = short_queries[...].astype(jnp.bfloat16)
    cands[my_shard, my_dp] = meta_ref[...]

    states = long_states[...]
    rows = pl.ds(0, long_count * seq_len)
    tiles = index_rows.shape[0] // LANES

    def turn(start, chunk):
        first = start * tiles // (3 * width)
        last = (start + chunk) * tiles // (3 * width)
        for tile in range(first, last):
            block = slice(tile * LANES, (tile + 1) * LANES)
            index_turned[:, block] = index_rows[block, :].T

    for part in range(3):
        project(states, qkv_weight, qkv_bias_ref, qkv_ref, rows, part, turn)
    pl.semaphore_wait(barrier, devices - 1)
    dp_start(1)
    dp_start(0)

    lane = lax.broadcasted_iota(jnp.int32, (1, LANES), 1)

    def text_step(text, carry):
        start = pl.multiple_of(text * seq_len, seq_len)
        text_len = jnp.sum(
            jnp.where(lane == LEN_LANE + short_count + text, meta_ref[half:, :], 0),
            axis=1,
            keepdims=True,
        )
        attend(qkv_ref, context_ref, start, seq_len, seq_len, text_len)
        here = pl.ds(start, seq_len)
        normed = normalise(long_states[here, :], context_ref[here, :], out_weight, out_bias_ref)
        row = lax.broadcasted_iota(jnp.int32, (seq_len, 1), 0)
        total = jnp.sum(jnp.where(row < text_len, normed, 0.0), axis=0, keepdims=True)
        query = embed(total, text_len.astype(jnp.float32), gain_ref, shift_ref)
        for piece in range(pieces):
            fold_ref[piece : piece + 1, :] = query[:, piece * LANES : (piece + 1) * LANES]
        long_queries[text, mine] = fold_ref[...].astype(jnp.bfloat16)
        all_start(text)

        @pl.when(text == 0)
        def _():
            for which in (1, 0):
                dp_settle(which, dp_recv)
                shard_start(which)

        return carry

    lax.fori_loop(0, long_count, text_step, 0)

    shard_settle(1, shard_recv)
    grouped = cands[...].reshape(devices, PACK, LANES)
    entry = lax.broadcasted_iota(jnp.int32, (1, compact), 1)
    block = entry % devices
    texts = ((block % dp_count) * shard_count + block // dp_count) * text_dev + entry // devices
    ids = jnp.concatenate(
        [grouped[:, half, rank : rank + 1] for rank in range(text_dev)], axis=0
    )
    pick_ref[...] = jnp.where(ids == texts, 1.0, 0.0).T.astype(jnp.bfloat16)
    shard_settle(0, shard_recv)
    for rank in range(short_count):
        unfold(queries[:, :, rank], rank, 1)
    for text in range(long_count - 1):
        all_settle(text, all_recv)
        unfold(long_queries[text], short_count + text, 1)
    first_part = picked(0, text_dev - 1)
    all_settle(long_count - 1, all_recv)
    unfold(long_queries[long_count - 1], text_dev - 1, 1)
    text_queries[...] = (first_part + picked(text_dev - 1, 1)).astype(jnp.bfloat16)

    rows_here = index_rows.shape[0]
    cand_count = LANES // 2
    local = jnp.concatenate([grouped[:, line, :] for line in range(half)], axis=0) - me * rows_here
    local = jnp.concatenate([local, pltpu.roll(local, cand_count, 1)], axis=0)
    group = local >> 7
    lane = local & (LANES - 1)
    total = jnp.zeros((compact, LANES), jnp.float32)
    rows_step = 1024
    for step in range(rows_here // rows_step):
        scores = jnp.dot(
            text_queries[...],
            index_turned[:, step * rows_step : (step + 1) * rows_step],
            preferred_element_type=jnp.float32,
        )
        for part in range(rows_step // LANES):
            found = jnp.take_along_axis(
                scores[:, part * LANES : (part + 1) * LANES],
                lane,
                axis=1,
                mode="promise_in_bounds",
            )
            total = jnp.where(group == step * (rows_step // LANES) + part, found, total)

    low = lax.broadcasted_iota(jnp.int32, (half * devices, LANES), 1) < cand_count
    packed = jnp.where(
        low, total[: half * devices], pltpu.roll(total[half * devices :], cand_count, 1)
    )
    for line in range(half):
        terms[:, line, :] = packed[line * devices : (line + 1) * devices]

    for far, off in everyone:
        pltpu.make_async_remote_copy(
            src_ref=terms.at[shard_peer(off) * dp_count + dp_peer(far)],
            dst_ref=arrived.at[far * shard_count + off],
            send_sem=out_send,
            recv_sem=out_recv,
            device_id=(dp_peer(far), shard_peer(off)),
            device_id_type=pl.DeviceIdType.MESH,
        ).start()
    for which in (0, 1):
        dp_settle(which, dp_send)
        shard_settle(which, shard_send)
    for text in range(long_count):
        all_settle(text, all_send)
    others = arrived.at[pl.ds(1, devices - 1)]
    settle(others, out_recv)
    result = terms[mine] + jnp.sum(others[...], axis=0)
    out_ref[:half, :] = result[:half, :cand_count]
    out_ref[half:, :] = result[:half, cand_count:]
    settle(others, out_send)


def shards(
    hidden,
    lengths,
    dealing,
    candidates,
    index_rows,
    qkv_weight,
    qkv_bias,
    out_weight,
    out_bias,
    norm_gain,
    norm_shift,
):
    text_dev, seq_len, width = hidden.shape
    dp_count, shard_count = lax.axis_size("dp"), lax.axis_size("shard")
    devices = dp_count * shard_count
    compact = devices * text_dev
    pieces = width // LANES
    hbm = pl.BlockSpec(memory_space=pl.ANY)
    vmem = pl.BlockSpec(memory_space=pltpu.VMEM)
    small = (qkv_bias[None, :], out_bias[None, :], norm_gain[None, :], norm_shift[None, :])
    long_count = text_dev // 3
    short_count = text_dev - long_count
    room, long_rows = short_count * seq_len, long_count * seq_len

    held = pl.pallas_call(
        functools.partial(encode_kernel, shard_count),
        in_specs=[hbm] * 11,
        out_specs=[vmem] * 10,
        out_shape=[
            pltpu.VMEM((short_count, pieces, LANES), jnp.float32),
            pltpu.VMEM((PACK, LANES), jnp.int32),
            pltpu.VMEM((1, 3 * width), jnp.float32),
            *[pltpu.VMEM((1, width), jnp.float32)] * 3,
            pltpu.VMEM((long_rows, width), jnp.bfloat16),
            pltpu.VMEM((width, 3 * width), jnp.bfloat16),
            pltpu.VMEM((width, width), jnp.bfloat16),
            pltpu.VMEM(index_rows.shape, jnp.bfloat16),
        ],
        scratch_shapes=[
            pltpu.VMEM((room, width), jnp.bfloat16),
            pltpu.VMEM((room, 3 * width), jnp.bfloat16),
            pltpu.VMEM((room, width), jnp.bfloat16),
            pltpu.VMEM((SLOTS, width), jnp.float32),
            pltpu.SMEM(lengths.shape, jnp.int32),
            pltpu.SMEM(dealing.shape, jnp.int32),
            pltpu.VMEM(candidates.shape, jnp.int32),
            pltpu.SemaphoreType.DMA((5,)),
            pltpu.SemaphoreType.DMA((text_dev,)),
            pltpu.SemaphoreType.DMA((7,)),
        ],
        compiler_params=pltpu.CompilerParams(vmem_limit_bytes=40 << 20),
        name="encode",
    )(lengths, dealing, candidates, *small, hidden, qkv_weight, out_weight, index_rows)

    return pl.pallas_call(
        functools.partial(finish_kernel, dp_count, shard_count),
        in_specs=[vmem] * 10,
        out_specs=vmem,
        out_shape=pltpu.VMEM(candidates.shape, jnp.float32),
        scratch_shapes=[
            pltpu.VMEM((width, index_rows.shape[0]), jnp.bfloat16),
            pltpu.VMEM((long_rows, 3 * width), jnp.bfloat16),
            pltpu.VMEM((long_rows, width), jnp.bfloat16),
            pltpu.VMEM((pieces, LANES), jnp.float32),
            pltpu.VMEM((shard_count, dp_count, short_count, pieces, LANES), jnp.bfloat16),
            pltpu.VMEM((long_count, devices, pieces, LANES), jnp.bfloat16),
            pltpu.VMEM((shard_count, dp_count, PACK, LANES), jnp.int32),
            pltpu.VMEM((compact, pieces, LANES), jnp.float32),
            pltpu.VMEM((compact, width), jnp.bfloat16),
            pltpu.VMEM((compact, width), jnp.bfloat16),
            pltpu.VMEM((compact, compact), jnp.bfloat16),
            pltpu.VMEM((devices, PACK, LANES), jnp.float32),
            pltpu.VMEM((devices, PACK, LANES), jnp.float32),
            *[pltpu.SemaphoreType.DMA((2,))] * 4,
            *[pltpu.SemaphoreType.DMA((long_count,))] * 2,
            *[pltpu.SemaphoreType.DMA] * 2,
        ],
        compiler_params=pltpu.CompilerParams(
            vmem_limit_bytes=40 << 20, collective_id=0, has_side_effects=True
        ),
        name="finish",
    )(*[pltpu.with_memory_space_constraint(x, pltpu.VMEM) for x in held])


def solution(mesh):
    in_specs = (
        P(("dp", "shard"), None, None),
        P(),
        P(),
        P(("dp", "shard"), None),
        P(("dp", "shard"), None),
        P(),
        P(),
        P(),
        P(),
        P(),
        P(),
    )
    out_specs = P(("dp", "shard"), None)
    return jax.shard_map(shards, mesh=mesh, in_specs=in_specs, out_specs=out_specs, check_vma=False)
```
